32 devices in a mesh: rep: 8 (over z, y), fsdp: 4 (over x, core).
Axes of the slice: x: 2, y: 2, z: 4, core: 2. Of those that a mesh axis runs over, the one named last changes fastest.
Arguments:
- inputs: bfloat16 [2, 32, 512, 1024], P(None, ('rep', 'fsdp')), may hold values from -6 to 6
- cotangent: bfloat16 [2, 32, 512, 1024], P(None, ('rep', 'fsdp')), may hold values from -6 to 6
- lengths: int32 [2, 32], P(None, ('rep', 'fsdp')), may hold values from 128 to 512, as said below
- pre_gain: bfloat16 [1024], P('fsdp'), may hold values from 0.5 to 1.5
- w_in: bfloat16 [1024, 4384], P('fsdp'), may hold values from -0.1875 to 0.1875
- conv_w: bfloat16 [4, 2304], P(None, 'fsdp'), may hold values from -3 to 3
- conv_b: bfloat16 [2304], P('fsdp'), may hold values from -3 to 3
- dt_bias: bfloat16 [32], P('fsdp'), may hold values from -6 to -3
- a_log: bfloat16 [32], P('fsdp'), may hold values from -1 to 2
- d_skip: bfloat16 [32], P('fsdp'), may hold values from 0.5 to 1.5
- norm_gain: bfloat16 [2048], P('fsdp'), may hold values from 0.5 to 1.5
- w_out: bfloat16 [2048, 1024], P('fsdp'), may hold values from -0.125 to 0.125
Outputs:
- result: bfloat16 [2, 32, 512, 1024], P(None, ('rep', 'fsdp'))
- grad_inputs: bfloat16 [2, 32, 512, 1024], P(None, ('rep', 'fsdp'))
- grad_pre_gain: float32 [1024], P('fsdp')
- grad_w_in: float32 [1024, 4384], P('fsdp')
- grad_conv_w: float32 [4, 2304], P(None, 'fsdp')
- grad_conv_b: float32 [2304], P('fsdp')
- grad_dt_bias: float32 [32], P('fsdp')
- grad_a_log: float32 [32], P('fsdp')
- grad_d_skip: float32 [32], P('fsdp')
- grad_norm_gain: float32 [2048], P('fsdp')
- grad_w_out: float32 [2048, 1024], P('fsdp')
The draws below stay inside these ranges and needn't reach their ends.
Inputs may be any that keep to these rules, and one draw needn't show every extreme that they name: `lengths`: each entry counts the valid leading slots of one sequence of 512 slots; every draw holds one sequence of exactly 512 and one of exactly 128.
All inputs are finite; a program needn't handle non-finite values.
Results may differ from the reference program's by a relative error of at most 0.0064.
Values may be sent and summed in bfloat16 or wider, within the bound.
No kernel may reach another device: no remote copies, remote signals or barrier semaphores. Data moves between devices by JAX's collectives and lax.ppermute only.
A program may use at most 256 MiB of HBM per device.

```python
import jax
import jax.numpy as jnp
from jax import lax

D = 1024
INNER = 2048
CONV = 4
BLOCK = 256
LEN = 512
MICRO = 2
HEADS = 32
XBC = 2304
PROJ = 4384
BATCH = 32


def draw_lengths(key, part):
    entries = MICRO * BATCH
    uniform_len = jax.random.randint(jax.random.fold_in(key, 11), (entries,), LEN // 4, LEN + 1)
    shuffled = jax.random.permutation(jax.random.fold_in(key, 12), entries)
    positions = jnp.arange(entries)
    lengths_flat = jnp.where(positions == shuffled[0], LEN, jnp.where(positions == shuffled[1], LEN // 4, uniform_len))
    return lengths_flat.reshape(MICRO, BATCH).astype(jnp.int32)


def steps_of(rng, shape, shards, smallest, high):
    loudness = 1.0
    for dim, parts in shards:
        heights = jax.random.uniform(jax.random.fold_in(jax.random.fold_in(rng, 6), dim), (parts,), jnp.float32, smallest / len(shards), high / len(shards))
        loudness = loudness * jnp.repeat(jnp.exp(heights), shape[dim] // parts).reshape((-1,) + (1,) * (len(shape) - 1 - dim))
    return loudness


def noise(key, extent, scale, reach, cuts=(), held_as=jnp.bfloat16):
    values = scale * jax.random.normal(key, extent, jnp.float32)
    if cuts:
        values = values * steps_of(key, extent, cuts, -0.22, 0.18)
    return jnp.clip(values, -reach, reach).astype(held_as)


def setup_inputs(seed: int = 0) -> dict:
    key_of = jax.random.split(jax.random.key(seed), 13)
    inputs = noise(key_of[0], (MICRO, BATCH, LEN, D), 1.0, 6.0, ((1, 32),))
    cotangent = noise(key_of[1], (MICRO, BATCH, LEN, D), 1.0, 6.0, ((1, 32),))
    lengths = draw_lengths(jax.random.fold_in(key_of[12], 71), 0)
    pre_gain = jnp.clip(1.0 + 0.1 * jax.random.normal(key_of[3], (D,), jnp.float32), 0.5, 1.5).astype(jnp.bfloat16)
    w_in = noise(key_of[4], (D, PROJ), D ** -0.5, 0.1875, ((0, 4),))
    conv_w = noise(key_of[5], (CONV, XBC), CONV ** -0.5, 3.0, ((1, 4),))
    conv_b = noise(key_of[6], (XBC,), 0.5, 3.0, ((0, 4),))
    dt_bias = jnp.clip(-6.0 + 3.0 * jax.random.uniform(key_of[7], (HEADS,), jnp.float32) ** steps_of(key_of[7], (HEADS,), ((0, 4),), -0.2, 0.2), -6.0, -3.0).astype(jnp.bfloat16)
    a_log = jnp.clip(-1.0 + 3.0 * jax.random.uniform(key_of[8], (HEADS,), jnp.float32) ** steps_of(key_of[8], (HEADS,), ((0, 4),), -0.2, 0.2), -1.0, 2.0).astype(jnp.bfloat16)
    d_skip = jnp.clip(0.5 + 1.0 * jax.random.uniform(key_of[9], (HEADS,), jnp.float32) ** steps_of(key_of[9], (HEADS,), ((0, 4),), -0.2, 0.2), 0.5, 1.5).astype(jnp.bfloat16)
    norm_gain = jnp.clip(1.0 + 0.1 * jax.random.normal(key_of[10], (INNER,), jnp.float32), 0.5, 1.5).astype(jnp.bfloat16)
    w_out = noise(key_of[11], (INNER, D), INNER ** -0.5, 0.125, ((0, 4),))
    return {"inputs": inputs, "cotangent": cotangent, "lengths": lengths, "pre_gain": pre_gain, "w_in": w_in, "conv_w": conv_w, "conv_b": conv_b, "dt_bias": dt_bias, "a_log": a_log, "d_skip": d_skip, "norm_gain": norm_gain, "w_out": w_out}


@jax.custom_vjp
def low(v):
    return lax.optimization_barrier(v.astype(jnp.bfloat16)).astype(jnp.float32)

@jax.custom_vjp
def low_back(v):
    return v

def low_keep(v):
    return (low(v), None)

def low_pass(kept, grad):
    return (grad,)

def back_keep(v):
    return (v, None)

def back_low(kept, grad):
    return (low(grad),)
low.defvjp(low_keep, low_pass)
low_back.defvjp(back_keep, back_low)
EPSILON = 1e-05
PRECISE = lax.Precision.HIGHEST

def rms_scale(values, gain_row):
    return values * lax.rsqrt(lax.optimization_barrier(jnp.mean(values * values, axis=-1, keepdims=True)) + EPSILON) * gain_row

def block_step(carry, pieces):
    hidden_state, a_neg = carry
    piece_x, piece_dt, piece_b, piece_c = pieces
    block_rows = piece_dt.shape[0]
    log_rates = piece_dt * a_neg[None, :]
    totals = jnp.cumsum(log_rates, axis=0)
    span_logs = totals[:, None, :] - totals[None, :, :]
    row_index = lax.broadcasted_iota(jnp.int32, (block_rows, block_rows, 1), 0)
    col_index = lax.broadcasted_iota(jnp.int32, (block_rows, block_rows, 1), 1)
    decay_table = jnp.exp(jnp.where(row_index >= col_index, span_logs, -jnp.inf))
    scores = jnp.dot(piece_c, piece_b.T, precision=PRECISE)
    weighted = piece_x * piece_dt[:, :, None]
    mixing = scores[:, :, None] * decay_table
    local_out = jnp.einsum('tsh,shp->thp', mixing, weighted, precision=PRECISE)
    carried = jnp.einsum('tn,hpn->thp', piece_c, hidden_state, precision=PRECISE) * jnp.exp(totals)[:, :, None]
    tail_decay = jnp.exp(totals[-1][None, :] - totals)
    update = jnp.einsum('shp,sn->hpn', weighted * tail_decay[:, :, None], piece_b, precision=PRECISE)
    new_state = jnp.exp(totals[-1])[:, None, None] * hidden_state + update
    return ((new_state, a_neg), local_out + carried)

def ssd_scan(heads_x, steps_dt, b_rows, c_rows, a_neg):
    seq_len, head_count, head_dim = heads_x.shape
    state_width = b_rows.shape[1]
    blocks = seq_len // BLOCK
    stacked = (heads_x.reshape(blocks, BLOCK, head_count, head_dim), steps_dt.reshape(blocks, BLOCK, head_count), b_rows.reshape(blocks, BLOCK, state_width), c_rows.reshape(blocks, BLOCK, state_width))
    zero_state = jnp.zeros((head_count, head_dim, state_width), jnp.float32)
    last_carry, outputs = lax.scan(jax.checkpoint(block_step), (zero_state, a_neg), stacked)
    return outputs.reshape(seq_len, head_count, head_dim)

def mixer(projected, conv_w, conv_b, dt_bias, a_log, d_skip, norm_gain):
    inner_width = norm_gain.shape[0]
    head_count = dt_bias.shape[0]
    channels = conv_b.shape[0]
    state_width = (channels - inner_width) // 2
    tap_count = conv_w.shape[0]
    seq_len = projected.shape[0]
    gate_part = projected[:, :inner_width]
    conv_in = projected[:, inner_width:inner_width + channels]
    dt_raw = projected[:, inner_width + channels:]
    padded = jnp.pad(conv_in, ((tap_count - 1, 0), (0, 0)))
    conv_out = conv_b[None, :] + conv_w[0][None, :] * padded[0:seq_len]
    for offset in range(1, tap_count):
        conv_out = conv_out + conv_w[offset][None, :] * padded[offset:offset + seq_len]
    active = jax.nn.silu(conv_out)
    heads_x = active[:, :inner_width].reshape(seq_len, head_count, inner_width // head_count)
    b_rows = active[:, inner_width:inner_width + state_width]
    c_rows = active[:, inner_width + state_width:]
    steps_dt = jax.nn.softplus(dt_raw + dt_bias[None, :])
    a_neg = -jnp.exp(a_log)
    mixed_rows = ssd_scan(heads_x, steps_dt, b_rows, c_rows, a_neg) + d_skip[None, :, None] * heads_x
    gated_rows = mixed_rows.reshape(seq_len, inner_width) * jax.nn.silu(gate_part)
    return rms_scale(gated_rows, norm_gain)

def block_forward(tokens, keep_mask, pre_gain, w_in, conv_w, conv_b, dt_bias, a_log, d_skip, norm_gain, w_out):
    normed = low(rms_scale(tokens, pre_gain))
    projected = low_back(jnp.dot(normed, w_in, precision=PRECISE))
    normed_mix = low(mixer(projected, conv_w, conv_b, dt_bias, a_log, d_skip, norm_gain))
    branch = low_back(jnp.dot(normed_mix, w_out, precision=PRECISE))
    return jnp.where(keep_mask, tokens + branch, 0.0)

def reference(inputs, cotangent, lengths, pre_gain, w_in, conv_w, conv_b, dt_bias, a_log, d_skip, norm_gain, w_out):
    params = tuple((weight_arr.astype(jnp.float32) for weight_arr in (pre_gain, w_in, conv_w, conv_b, dt_bias, a_log, d_skip, norm_gain, w_out)))
    seq_count = inputs.shape[0] * inputs.shape[1]
    seq_len = inputs.shape[2]
    model_width = inputs.shape[3]
    flat_inputs = inputs.reshape(seq_count, seq_len, model_width)
    flat_cot = cotangent.reshape(seq_count, seq_len, model_width)
    flat_lengths = lengths.reshape(seq_count)

    def per_sequence(grads, pieces):
        tokens, cot_rows, length_now = pieces
        keep_mask = lax.broadcasted_iota(jnp.int32, (seq_len, 1), 0) < length_now
        tokens_f = tokens.astype(jnp.float32)
        outcome, pullback = jax.vjp(lambda token_rows, *weights: block_forward(token_rows, keep_mask, *weights), tokens_f, *params)
        pulled = pullback(cot_rows.astype(jnp.float32))
        grads = tuple((old_grad + new_grad for old_grad, new_grad in zip(grads, pulled[1:])))
        return (grads, (outcome.astype(jnp.bfloat16), pulled[0].astype(jnp.bfloat16)))
    zero_grads = tuple((jnp.zeros_like(weight_arr) for weight_arr in params))
    grads, (outcomes, input_grads) = lax.scan(per_sequence, zero_grads, (flat_inputs, flat_cot, flat_lengths))
    return (outcomes.reshape(inputs.shape), input_grads.reshape(inputs.shape), grads[0], grads[1], grads[2], grads[3], grads[4], grads[5], grads[6], grads[7], grads[8])
```

```python
import functools

import jax
import jax.numpy as jnp
from jax import lax
from jax.experimental import pallas as pl
from jax.experimental.pallas import tpu as pltpu
from jax.sharding import PartitionSpec as P

EPSILON = 1e-05
PRECISE = lax.Precision.HIGHEST
CHUNK = 128
GROUP = 8
LANES = 128
LOG2E = 1.4426950408889634
F32 = jnp.float32
BF16 = jnp.bfloat16


def dot_nn(a, b):
    return lax.dot_general(a, b, (((1,), (0,)), ((), ())), preferred_element_type=F32)


def dot_nt(a, b):
    return lax.dot_general(a, b, (((1,), (1,)), ((), ())), preferred_element_type=F32)


def dot_tn(a, b):
    return lax.dot_general(a, b, (((0,), (0,)), ((), ())), preferred_element_type=F32)


def sigmoid(v):
    return 1.0 / (1.0 + jnp.exp(-v))


def split_two(v):
    high = v.astype(BF16)
    return high, (v - high.astype(F32)).astype(BF16)


def head_rows(width, count):
    per = width // count
    row = lax.broadcasted_iota(jnp.int32, (count, width), 0)
    lane = lax.broadcasted_iota(jnp.int32, (count, width), 1)
    return jnp.where(lane // per == row, 1.0, 0.0).astype(BF16)


def spread_heads(values, ones_rows):
    high, low = split_two(values)
    return dot_tn(jnp.concatenate([high, low], 0), jnp.concatenate([ones_rows, ones_rows], 0))


def sum_heads(values, ones_rows):
    high, low = split_two(values)
    return dot_nt(ones_rows, high) + dot_nt(ones_rows, low)


def window_before(ref, chunk, lanes):
    start = pl.multiple_of(chunk * CHUNK, CHUNK)
    before = pl.multiple_of(jnp.maximum(start - 8, 0), 8)
    halo = jnp.where(chunk > 0, ref[pl.ds(before, 8), lanes], 0.0)
    return jnp.concatenate([halo, ref[pl.ds(start, CHUNK), lanes]], 0)


def taps_of(window, tap_count):
    return [window[8:]] + [pltpu.roll(window, back, 0)[8:] for back in range(1, tap_count)]


def conv_of(shifted, conv_w, conv_b):
    last = conv_w.shape[0] - 1
    total = conv_b
    for back, rows in enumerate(shifted):
        total = total + conv_w[last - back : last - back + 1] * rows
    return total


def pair_blocks(pair):
    lane = lax.broadcasted_iota(jnp.int32, pair.shape, 1)
    half = pair.shape[1] // 2
    zero = jnp.zeros_like(pair)
    return jnp.concatenate([jnp.where(lane < half, pair, zero), jnp.where(lane < half, zero, pair)], 0)


def step_tables(dt_raw, dt_bias, a_neg):
    shifted = dt_raw + dt_bias
    steps = jnp.maximum(shifted, 0.0) + jnp.log1p(jnp.exp(-jnp.abs(shifted)))
    rates = steps * a_neg
    row = lax.broadcasted_iota(jnp.int32, (CHUNK, CHUNK), 0)
    col = lax.broadcasted_iota(jnp.int32, (CHUNK, CHUNK), 1)
    upper = jnp.where(row <= col, 1.0, 0.0).astype(F32)
    totals = lax.dot_general(
        rates, upper, (((1,), (0,)), ((), ())), precision=PRECISE, preferred_element_type=F32
    )
    return shifted, steps, totals * LOG2E


def prepare(c, bc_ref, dt_ref, cw_ref, cb_ref, small_ref, heads, bcs, gs, tcol, rvt, e1t, e2t, keep=None):
    rows = pl.ds(pl.multiple_of(c * CHUNK, CHUNK), CHUNK)
    for lanes in (slice(0, 128), slice(128, 256)):
        shifted = taps_of(window_before(bc_ref, c, lanes), cw_ref.shape[0])
        conv_out = conv_of(shifted, cw_ref[:, lanes], cb_ref[:, lanes])
        bcs[rows, lanes] = (conv_out * sigmoid(conv_out)).astype(BF16)
    b_rows = bcs[rows, 0:128]
    c_rows = bcs[rows, 128:256]
    gs[rows, :] = dot_nt(c_rows, b_rows)
    dt_raw = dt_ref[rows, :].T[:heads]
    shifted, steps, totals = step_tables(dt_raw, small_ref[:, 0:1], small_ref[:, 1:2])
    below = jnp.log2(steps) - totals
    pad = jnp.zeros((LANES - heads, CHUNK), F32)
    tcol[rows, :] = jnp.concatenate([totals, pad], 0).T
    rvt[c] = below
    e1t[c] = jnp.exp2(totals)
    e2t[c] = jnp.exp2(totals[:, CHUNK - 1 :] + below)
    if keep is not None:
        keep(c, shifted, steps)


def decay_of(totals_col, below_row):
    row = lax.broadcasted_iota(jnp.int32, (CHUNK, CHUNK), 0)
    col = lax.broadcasted_iota(jnp.int32, (CHUNK, CHUNK), 1)
    return jnp.exp2(jnp.where(row >= col, totals_col + below_row, -jnp.inf))


def columns_of(tcol_chunk, group, groups):
    shift = lax.rem(LANES - group * GROUP, LANES)
    return pltpu.roll(tcol_chunk, shift, 1)


def scan_forward(
    x_ref, bc_ref, dt_ref, cwx_ref, cbx_ref, cwb_ref, cbb_ref, small_ref, skip_ref,
    mixed_ref, states_ref,
    bcs, gs, tcol, rvt, e1t, e2t, state, xe2,
    *, heads,
):
    group = pl.program_id(1)
    chunks = x_ref.shape[0] // CHUNK
    width = x_ref.shape[1]
    ones_rows = head_rows(width, GROUP)

    @pl.when(group == 0)
    def _():
        def one(c, carry):
            prepare(c, bc_ref, dt_ref, cwb_ref, cbb_ref, small_ref, heads, bcs, gs, tcol, rvt, e1t, e2t)
            return carry

        lax.fori_loop(0, chunks, one, 0)

    state[...] = jnp.zeros_like(state)

    def chunk_step(c, carry):
        rows = pl.ds(pl.multiple_of(c * CHUNK, CHUNK), CHUNK)
        mine = pl.ds(pl.multiple_of(group * GROUP, GROUP), GROUP)
        e1 = spread_heads(e1t[c, mine, :], ones_rows)
        e2 = spread_heads(e2t[c, mine, :], ones_rows)
        below = rvt[c, mine, :]
        columns = columns_of(tcol[rows, :], group, 0)
        scores = gs[rows, :]
        state_now = state[...]
        state_b = state_now.astype(BF16)
        states_ref[0, c] = state_b
        carried = dot_nn(bcs[rows, 128:256], state_b) * e1
        for pair in range(width // LANES):
            lanes = slice(pair * LANES, (pair + 1) * LANES)
            shifted = taps_of(window_before(x_ref, c, lanes), cwx_ref.shape[0])
            conv_out = conv_of(shifted, cwx_ref[:, lanes], cbx_ref[:, lanes])
            x = conv_out * sigmoid(conv_out)
            mixing = []
            for head in (2 * pair, 2 * pair + 1):
                decay = decay_of(columns[:, head : head + 1], below[head : head + 1])
                mixing.append((scores * decay).astype(BF16))
            local = dot_nn(jnp.concatenate(mixing, 1), pair_blocks(x.astype(BF16)))
            mixed_ref[rows, lanes] = local + carried[:, lanes] + skip_ref[:, lanes] * x
            xe2[:, lanes] = (x * e2[:, lanes]).astype(BF16)
        state[...] = e1[CHUNK - 1 :] * state_now + dot_tn(bcs[rows, 0:128], xe2[...])
        return carry

    lax.fori_loop(0, chunks, chunk_step, 0)


def gate_kernel(
    lengths_ref, normed_ref, cot_ref, tok_ref, mixed_ref, wg_ref, wo_ref, gain_ref,
    nm_ref, dy_ref, gg_ref, res_ref, r1_ref, ggain_ref,
    gate, gnm, sig,
    *, heads, seq_len,
):
    step = pl.program_id(0)
    rows = normed_ref.shape[0]
    inner = mixed_ref.shape[1]
    blocks = seq_len // rows
    length = lengths_ref[step // blocks]
    slot = lax.rem(step, blocks) * rows + lax.broadcasted_iota(jnp.int32, (rows, 1), 0)
    keep = slot < length
    cot_b = jnp.where(keep, cot_ref[...].astype(F32), 0.0).astype(BF16)
    normed = normed_ref[...]
    squares = jnp.zeros((rows, LANES), F32)
    dots = jnp.zeros((rows, LANES), F32)
    wide = 512
    for start in range(0, inner, wide):
        part = slice(start, start + wide)
        gate[:, part] = dot_nn(normed, wg_ref[:, part])
        gnm[:, part] = dot_nt(cot_b, wo_ref[part, :])
        for lane in range(start, start + wide, LANES):
            lanes = slice(lane, lane + LANES)
            g = gate[:, lanes]
            s = sigmoid(g)
            sig[:, lanes] = s
            gated = mixed_ref[:, lanes] * (g * s)
            squares = squares + gated * gated
            dots = dots + gnm[:, lanes] * gain_ref[:, lanes] * gated
    r = lax.rsqrt(jnp.sum(squares, 1, keepdims=True) / inner + EPSILON)
    mean = r * (jnp.sum(dots, 1, keepdims=True) / inner)

    @pl.when(step == 0)
    def _():
        ggain_ref[...] = jnp.zeros_like(ggain_ref)

    r1 = jnp.zeros((heads, rows), F32)
    per = inner // heads
    for start in range(0, inner, wide):
        for lane in range(start, start + wide, LANES):
            lanes = slice(lane, lane + LANES)
            g = gate[:, lanes]
            s = sig[:, lanes]
            m = mixed_ref[:, lanes]
            gain = gain_ref[:, lanes]
            up = gnm[:, lanes]
            silu = g * s
            unit = m * silu * r
            ggated = r * (up * gain - unit * mean)
            dy = (ggated * silu).astype(BF16)
            dy_ref[:, lanes] = dy
            gg_ref[:, lanes] = (ggated * m * (s + silu * (1.0 - s))).astype(BF16)
            nm_ref[:, lanes] = (unit * gain).astype(BF16)
            ggain_ref[0:1, lanes] += jnp.sum(up * unit, 0, keepdims=True)
            row = lax.broadcasted_iota(jnp.int32, (heads, LANES), 0)
            col = lax.broadcasted_iota(jnp.int32, (heads, LANES), 1) + lane
            ones_rows = jnp.where(col // per == row, 1.0, 0.0).astype(BF16)
            r1 = r1 + sum_heads(dy.astype(F32) * m, ones_rows)
    r1_ref[0] = r1
    half = wo_ref.shape[1] // 2
    for start in (0, half):
        part = slice(start, start + half)
        branch = dot_nn(nm_ref[...], wo_ref[:, part])
        res_ref[:, part] = jnp.where(keep, tok_ref[:, part].astype(F32) + branch, 0.0).astype(BF16)


def conv_back(grad, halo, conv_w):
    last = conv_w.shape[0] - 1
    window = jnp.concatenate([grad, halo], 0)
    total = conv_w[last:] * grad
    size = window.shape[0]
    for ahead in range(1, last + 1):
        total = total + conv_w[last - ahead : last - ahead + 1] * pltpu.roll(window, size - ahead, 0)[:CHUNK]
    return total


def add_tap_grads(out_ref, lanes, grad, shifted):
    last = len(shifted) - 1
    for back, rows in enumerate(shifted):
        tap = last - back
        out_ref[0, tap : tap + 1, lanes] += jnp.sum(grad * rows, 0, keepdims=True)
    out_ref[0, last + 1 : last + 2, lanes] += jnp.sum(grad, 0, keepdims=True)


def scan_backward(
    x_ref, bc_ref, dt_ref, dy_ref, states_ref, r1_ref, cwx_ref, cbx_ref, cwb_ref, cbb_ref, small_ref, skip_ref,
    gx_ref, gbcdt_ref, convx_ref, convb_ref, heads_ref,
    bcs, gs, tcol, rvt, e1t, e2t, shs, sts, adj, xe2, hs, dgs, dbs, dcs, halo, halo_b, colz, vsum, r2s, ends,
    *, heads,
):
    group = pl.program_id(1)
    groups = pl.num_programs(1)
    chunks = x_ref.shape[0] // CHUNK
    width = x_ref.shape[1]
    ones_rows = head_rows(width, GROUP)
    mine = pl.ds(pl.multiple_of(group * GROUP, GROUP), GROUP)

    @pl.when(group == 0)
    def _():
        def keep(c, shifted, steps):
            shs[c] = shifted
            sts[c] = steps

        def one(c, carry):
            prepare(c, bc_ref, dt_ref, cwb_ref, cbb_ref, small_ref, heads, bcs, gs, tcol, rvt, e1t, e2t, keep)
            return carry

        lax.fori_loop(0, chunks, one, 0)
        dgs[...] = jnp.zeros_like(dgs)
        dbs[...] = jnp.zeros_like(dbs)
        dcs[...] = jnp.zeros_like(dcs)

    adj[...] = jnp.zeros_like(adj)
    halo[...] = jnp.zeros_like(halo)
    convx_ref[...] = jnp.zeros_like(convx_ref)

    def chunk_step(i, carry):
        c = chunks - 1 - i
        rows = pl.ds(pl.multiple_of(c * CHUNK, CHUNK), CHUNK)
        e1 = spread_heads(e1t[c, mine, :], ones_rows)
        e2 = spread_heads(e2t[c, mine, :], ones_rows)
        below = rvt[c, mine, :]
        columns = columns_of(tcol[rows, :], group, 0)
        scores = gs[rows, :]
        adj_now = adj[...]
        adj_b = adj_now.astype(BF16)
        state_b = states_ref[0, c]
        b_rows = bcs[rows, 0:128]
        c_rows = bcs[rows, 128:256]
        from_adj = dot_nn(b_rows, adj_b) * e2
        cross = e1[CHUNK - 1 :] * jnp.sum(adj_now * state_b.astype(F32), 0, keepdims=True)
        dg = dgs[rows, :]
        col_total = jnp.zeros((GROUP, CHUNK), F32)
        v_total = jnp.zeros((GROUP, CHUNK), F32)
        r2_total = jnp.zeros((GROUP, CHUNK), F32)
        for pair in range(width // LANES):
            lanes = slice(pair * LANES, (pair + 1) * LANES)
            shifted = taps_of(window_before(x_ref, c, lanes), cwx_ref.shape[0])
            conv_out = conv_of(shifted, cwx_ref[:, lanes], cbx_ref[:, lanes])
            s = sigmoid(conv_out)
            x = conv_out * s
            xb = x.astype(BF16)
            dyb = dy_ref[rows, lanes]
            dy = dyb.astype(F32)
            both = dot_nt(dyb, pair_blocks(xb))
            mixing = []
            for k, head in enumerate((2 * pair, 2 * pair + 1)):
                decay = decay_of(columns[:, head : head + 1], below[head : head + 1])
                mixing.append((scores * decay).astype(BF16))
                dg = dg + both[:, k * CHUNK : (k + 1) * CHUNK] * decay
            local = dot_tn(jnp.concatenate(mixing, 0), pair_blocks(dyb))
            tail = from_adj[:, lanes]
            dx = local + tail + skip_ref[:, lanes] * dy
            grad = dx * (s + x * (1.0 - s))
            gx_ref[rows, lanes] = conv_back(grad, halo[:, lanes], cwx_ref[:, lanes]).astype(BF16)
            halo[:, lanes] = grad[:8]
            add_tap_grads(convx_ref, lanes, grad, shifted)
            hs[:, lanes] = (dy * e1[:, lanes]).astype(BF16)
            xe2[:, lanes] = (x * e2[:, lanes]).astype(BF16)
            pair_ones = ones_rows[:, lanes]
            col_total = col_total + sum_heads(xb.astype(F32) * local, pair_ones)
            v_total = v_total + sum_heads(x * tail, pair_ones)
            r2_total = r2_total + sum_heads(dy * x, pair_ones)
        dgs[rows, :] = dg
        colz[c, mine, :] = col_total
        vsum[c, mine, :] = v_total
        r2s[c, mine, :] = r2_total
        ends[c, mine, :] = jnp.broadcast_to(
            sum_heads(jnp.broadcast_to(cross, (8, width)), ones_rows)[:, 0:1], (GROUP, CHUNK)
        )
        dcs[rows, :] += dot_nt(hs[...], state_b)
        dbs[rows, :] += dot_nt(xe2[...], adj_b)
        adj[...] = e1[CHUNK - 1 :] * adj_now + dot_tn(c_rows, hs[...])
        return carry

    lax.fori_loop(0, chunks, chunk_step, 0)

    @pl.when(group == groups - 1)
    def _():
        convb_ref[...] = jnp.zeros_like(convb_ref)
        heads_ref[...] = jnp.zeros_like(heads_ref)
        halo_b[...] = jnp.zeros_like(halo_b)
        row = lax.broadcasted_iota(jnp.int32, (CHUNK, CHUNK), 0)
        col = lax.broadcasted_iota(jnp.int32, (CHUNK, CHUNK), 1)
        later = jnp.where(row >= col, 1.0, 0.0).astype(F32)
        earlier = jnp.where(row < col, 1.0, 0.0).astype(F32)

        def finish(i, carry):
            c = chunks - 1 - i
            rows = pl.ds(pl.multiple_of(c * CHUNK, CHUNK), CHUNK)
            dg = dgs[rows, :].astype(BF16)
            b_rows = bcs[rows, 0:128]
            c_rows = bcs[rows, 128:256]
            totals = (dbs[rows, :] + dot_tn(dg, c_rows), dcs[rows, :] + dot_nn(dg, b_rows))
            for lanes, total in zip((slice(0, 128), slice(128, 256)), totals):
                shifted = taps_of(window_before(bc_ref, c, lanes), cwb_ref.shape[0])
                conv_out = conv_of(shifted, cwb_ref[:, lanes], cbb_ref[:, lanes])
                s = sigmoid(conv_out)
                grad = total * (s + conv_out * s * (1.0 - s))
                gbcdt_ref[rows, lanes] = conv_back(grad, halo_b[:, lanes], cwb_ref[:, lanes]).astype(BF16)
                halo_b[:, lanes] = grad[:8]
                add_tap_grads(convb_ref, lanes, grad, shifted)
            a_neg = small_ref[:, 1:2]
            skip = small_ref[:, 2:3]
            inner_part = r1_ref[c] - skip * r2s[c] - colz[c]
            dims = (((1,), (0,)), ((), ()))
            q = (
                lax.dot_general(inner_part, later, dims, precision=PRECISE, preferred_element_type=F32)
                + lax.dot_general(vsum[c], earlier, dims, precision=PRECISE, preferred_element_type=F32)
                + ends[c]
            )
            shifted_dt = shs[c]
            steps = sts[c]
            sig = sigmoid(shifted_dt)
            ratio = jnp.where(shifted_dt < -15.0, 1.0, sig / steps)
            grad_dt = ratio * (colz[c] + vsum[c]) + sig * a_neg * q
            pad = jnp.zeros((LANES - heads, CHUNK), F32)
            gbcdt_ref[rows, 256:384] = jnp.concatenate([grad_dt, pad], 0).T.astype(BF16)
            heads_ref[0, :, 0:1] += jnp.sum(grad_dt, 1, keepdims=True)
            heads_ref[0, :, 1:2] += a_neg * jnp.sum(steps * q, 1, keepdims=True)
            heads_ref[0, :, 2:3] += jnp.sum(r2s[c], 1, keepdims=True)
            return carry

        lax.fori_loop(0, chunks, finish, 0)


def params(limit_mib=56):
    return pltpu.CompilerParams(vmem_limit_bytes=limit_mib * 2**20, dimension_semantics=None)


def scan_specs(seq_len, width, inner, taps):
    whole = lambda *shape: pl.BlockSpec(shape, lambda m, g: (0,) * len(shape))
    return dict(
        x=pl.BlockSpec((seq_len, width), lambda m, g: (m, g)),
        bc=pl.BlockSpec((seq_len, 256), lambda m, g: (m, inner // 256)),
        dt=pl.BlockSpec((seq_len, LANES), lambda m, g: (m, inner // LANES + 2)),
        cwx=pl.BlockSpec((taps, width), lambda m, g: (0, g)),
        cbx=pl.BlockSpec((1, width), lambda m, g: (0, g)),
        cwb=whole(taps, 256),
        cbb=whole(1, 256),
        skip=pl.BlockSpec((1, width), lambda m, g: (0, g)),
    )


def table_scratch(seq_len, heads):
    chunks = seq_len // CHUNK
    return [
        pltpu.VMEM((seq_len, 256), BF16),
        pltpu.VMEM((seq_len, CHUNK), F32),
        pltpu.VMEM((seq_len, LANES), F32),
        pltpu.VMEM((chunks, heads, CHUNK), F32),
        pltpu.VMEM((chunks, heads, CHUNK), F32),
        pltpu.VMEM((chunks, heads, CHUNK), F32),
    ]


def call_forward(rest, conv_w, conv_b, small, skip_row, seq_count, inner, heads):
    seq_len = rest.shape[0] // seq_count
    width = GROUP * (inner // heads)
    chunks = seq_len // CHUNK
    taps = conv_w.shape[0]
    sp = scan_specs(seq_len, width, inner, taps)
    return pl.pallas_call(
        functools.partial(scan_forward, heads=heads),
        grid=(seq_count, inner // width),
        in_specs=[sp["x"], sp["bc"], sp["dt"], sp["cwx"], sp["cbx"], sp["cwb"], sp["cbb"],
                  pl.BlockSpec(small.shape, lambda m, g: (0, 0)), sp["skip"]],
        out_specs=[pl.BlockSpec((seq_len, width), lambda m, g: (m, g)),
                   pl.BlockSpec((1, chunks, 128, width), lambda m, g: (m, 0, 0, g))],
        out_shape=[jax.ShapeDtypeStruct((rest.shape[0], inner), F32),
                   jax.ShapeDtypeStruct((seq_count, chunks, 128, inner), BF16)],
        scratch_shapes=table_scratch(seq_len, heads) + [
            pltpu.VMEM((128, width), F32),
            pltpu.VMEM((CHUNK, width), BF16),
        ],
        compiler_params=params(),
        name="scan_forward",
    )(rest, rest, rest, conv_w[:, :inner], conv_b[:, :inner], conv_w[:, inner:], conv_b[:, inner:], small, skip_row)


def call_gate(lengths, normed, cot, tokens, mixed, w_gate, w_out, gain, heads, seq_len):
    total, width = normed.shape
    inner = mixed.shape[1]
    rows = CHUNK
    steps = total // rows
    blk = lambda w: pl.BlockSpec((rows, w), lambda i, _: (i, 0))
    whole = lambda *shape: pl.BlockSpec(shape, lambda i, _: (0,) * len(shape))
    return pl.pallas_call(
        functools.partial(gate_kernel, heads=heads, seq_len=seq_len),
        grid_spec=pltpu.PrefetchScalarGridSpec(
            num_scalar_prefetch=1,
            grid=(steps,),
            in_specs=[blk(width), blk(width), blk(width), blk(inner), whole(*w_gate.shape), whole(*w_out.shape),
                      whole(1, inner)],
            out_specs=[blk(inner), blk(inner), blk(inner), blk(width),
                       pl.BlockSpec((1, heads, rows), lambda i, _: (i, 0, 0)), whole(8, inner)],
            scratch_shapes=[pltpu.VMEM((rows, inner), F32)] * 3,
        ),
        out_shape=[jax.ShapeDtypeStruct((total, inner), BF16)] * 3 + [
            jax.ShapeDtypeStruct((total, width), BF16),
            jax.ShapeDtypeStruct((steps, heads, rows), F32),
            jax.ShapeDtypeStruct((8, inner), F32)],
        compiler_params=params(),
        name="gate",
    )(lengths, normed, cot, tokens, mixed, w_gate, w_out, gain)


def call_backward(rest, dy, states, r1, conv_w, conv_b, small, skip_row, seq_count, inner, heads):
    seq_len = rest.shape[0] // seq_count
    width = GROUP * (inner // heads)
    chunks = seq_len // CHUNK
    taps = conv_w.shape[0]
    sp = scan_specs(seq_len, width, inner, taps)
    table = lambda: pltpu.VMEM((chunks, heads, CHUNK), F32)
    return pl.pallas_call(
        functools.partial(scan_backward, heads=heads),
        grid=(seq_count, inner // width),
        in_specs=[sp["x"], sp["bc"], sp["dt"],
                  pl.BlockSpec((seq_len, width), lambda m, g: (m, g)),
                  pl.BlockSpec((1, chunks, 128, width), lambda m, g: (m, 0, 0, g)),
                  pl.BlockSpec((chunks, heads, CHUNK), lambda m, g: (m, 0, 0)),
                  sp["cwx"], sp["cbx"], sp["cwb"], sp["cbb"],
                  pl.BlockSpec(small.shape, lambda m, g: (0, 0)), sp["skip"]],
        out_specs=[pl.BlockSpec((seq_len, width), lambda m, g: (m, g)),
                   pl.BlockSpec((seq_len, 384), lambda m, g: (m, 0)),
                   pl.BlockSpec((1, 8, width), lambda m, g: (m, 0, g)),
                   pl.BlockSpec((1, 8, 256), lambda m, g: (m, 0, 0)),
                   pl.BlockSpec((1, heads, LANES), lambda m, g: (m, 0, 0))],
        out_shape=[jax.ShapeDtypeStruct((rest.shape[0], inner), BF16),
                   jax.ShapeDtypeStruct((rest.shape[0], 384), BF16),
                   jax.ShapeDtypeStruct((seq_count, 8, inner), F32),
                   jax.ShapeDtypeStruct((seq_count, 8, 256), F32),
                   jax.ShapeDtypeStruct((seq_count, heads, LANES), F32)],
        scratch_shapes=table_scratch(seq_len, heads) + [
            table(), table(),
            pltpu.VMEM((128, width), F32),
            pltpu.VMEM((CHUNK, width), BF16),
            pltpu.VMEM((CHUNK, width), BF16),
            pltpu.VMEM((seq_len, CHUNK), F32),
            pltpu.VMEM((seq_len, 128), F32),
            pltpu.VMEM((seq_len, 128), F32),
            pltpu.VMEM((8, width), F32),
            pltpu.VMEM((8, 256), F32),
            table(), table(), table(), table(),
        ],
        compiler_params=params(),
        name="scan_backward",
    )(rest, rest, rest, dy, states, r1, conv_w[:, :inner], conv_b[:, :inner], conv_w[:, inner:], conv_b[:, inner:],
      small, skip_row)


def rms_parts(tokens):
    scale = lax.rsqrt(jnp.mean(tokens * tokens, axis=-1, keepdims=True) + EPSILON)
    return tokens * scale, scale


def on_device(
    inputs, cotangent, lengths, pre_gain, w_in, conv_w, conv_b, dt_bias, a_log, d_skip, norm_gain, w_out
):
    micro, seqs, seq_len, width = inputs.shape
    seq_count = micro * seqs
    rows = seq_count * seq_len
    gather = lambda v, axis: lax.all_gather(v, "fsdp", axis=axis, tiled=True)
    inner = norm_gain.shape[0] * lax.axis_size("fsdp")
    pad = (-w_in.shape[1]) % LANES
    rest_shard = jnp.pad(w_in[:, inner:], ((0, 0), (0, pad)))
    w_rest = gather(rest_shard, 0)
    w_gate = gather(w_in[:, :inner], 0)
    wo = gather(w_out, 0)
    smalls = [gather(v, v.ndim - 1).astype(F32) for v in (pre_gain, conv_w, conv_b, dt_bias, a_log, d_skip, norm_gain)]
    pre, cw, cb, dtb, alog, skip, ngain = smalls
    heads = dtb.shape[0]
    a_neg = -jnp.exp(alog)
    small = jnp.pad(jnp.stack([dtb, a_neg, skip], 1), ((0, 0), (0, LANES - 3)))
    skip_row = jnp.repeat(skip, inner // heads)[None]
    tokens = inputs.reshape(rows, width)
    cot = cotangent.reshape(rows, width)
    flat_lengths = lengths.reshape(seq_count)
    unit0, r0 = rms_parts(tokens.astype(F32))
    normed = (unit0 * pre).astype(BF16)
    rest = jnp.dot(normed, w_rest, preferred_element_type=F32)
    mixed, states = call_forward(rest, cw, cb[None], small, skip_row, seq_count, inner, heads)
    nm, dy, gg, res, r1, ggain = call_gate(
        flat_lengths, normed, cot, tokens, mixed, w_gate, wo, ngain[None], heads, seq_len
    )
    keep = (lax.broadcasted_iota(jnp.int32, (seq_count, seq_len, 1), 1) < flat_lengths[:, None, None]).reshape(rows, 1)
    grad_res = jnp.where(keep, cot.astype(F32), 0.0)
    grad_branch = grad_res.astype(BF16)
    gw_out = dot_tn(nm, grad_branch)
    gw_gate = dot_tn(normed, gg)
    gx, gbcdt, convx, convb, headg = call_backward(
        rest, dy, states, r1, cw, cb[None], small, skip_row, seq_count, inner, heads
    )
    gw_x = dot_tn(normed, gx)
    gw_bcdt = dot_tn(normed, gbcdt)
    grad_normed = dot_nt(gg, w_gate) + dot_nt(gx, w_rest[:, :inner]) + dot_nt(gbcdt, w_rest[:, inner:])
    up = grad_normed * pre
    grad_pre = jnp.sum(grad_normed * unit0, 0)
    grad_tokens = r0 * (up - unit0 * jnp.mean(up * unit0, axis=-1, keepdims=True))
    grad_in = (grad_res + grad_tokens).astype(BF16)
    gw_in = jnp.concatenate([gw_gate, gw_x, gw_bcdt[:, : w_in.shape[1] - 2 * inner]], 1)
    taps = cw.shape[0]
    conv_all = jnp.concatenate([jnp.sum(convx, 0), jnp.sum(convb, 0)], 1)
    headg = jnp.sum(headg, 0)
    scatter = lambda v, axis: lax.psum_scatter(v, "fsdp", scatter_dimension=axis, tiled=True)
    shares = (
        scatter(grad_pre, 0), scatter(gw_in, 0), scatter(conv_all[:taps], 1), scatter(conv_all[taps], 0),
        scatter(headg[:, 0], 0), scatter(headg[:, 1], 0), scatter(headg[:, 2], 0), scatter(ggain[0], 0),
        scatter(gw_out, 0),
    )
    summed = lax.psum(shares, "rep")
    return (res.reshape(inputs.shape), grad_in.reshape(inputs.shape)) + tuple(summed)


def solution(mesh):
    data = P(None, ("rep", "fsdp"), None, None)
    vec = P("fsdp")
    in_specs = (data, data, P(None, ("rep", "fsdp")), vec, P("fsdp", None), P(None, "fsdp"), vec, vec, vec, vec, vec,
                P("fsdp", None))
    out_specs = (data, data, vec, P("fsdp", None), P(None, "fsdp"), vec, vec, vec, vec, vec, P("fsdp", None))
    return jax.shard_map(on_device, mesh=mesh, in_specs=in_specs, out_specs=out_specs, check_vma=False)
```

```python
import functools

import jax
import jax.numpy as jnp
from jax import lax
from jax.experimental import pallas as pl
from jax.experimental.pallas import tpu as pltpu
from jax.sharding import PartitionSpec as P


EPSILON = 1e-05
PRECISE = lax.Precision.HIGHEST
CHUNK = 128
GROUP = 8
LANES = 128
LOG2E = 1.4426950408889634
BIAS_ROW = 4
PRE_ROW = 5
GAIN_ROW = 6
VMEM_BYTES = 67043328
WIDE = 512
GATE_ROWS = 256
SPLIT = 2
FIRST_OF = {True: 0, False: SPLIT}
F32 = jnp.float32
BF16 = jnp.bfloat16


def dot_nn(a, b):
    return lax.dot_general(a, b, (((1,), (0,)), ((), ())), preferred_element_type=F32)


def dot_nt(a, b):
    return lax.dot_general(a, b, (((1,), (1,)), ((), ())), preferred_element_type=F32)


def dot_tn(a, b):
    return lax.dot_general(a, b, (((0,), (0,)), ((), ())), preferred_element_type=F32)


def sigmoid(v):
    return 1.0 / (1.0 + jnp.exp(-v))


def split_two(v):
    high = v.astype(BF16)
    return high, (v - high.astype(F32)).astype(BF16)


def head_rows(width, count):
    per = width // count
    row = lax.broadcasted_iota(jnp.int32, (count, width), 0)
    lane = lax.broadcasted_iota(jnp.int32, (count, width), 1)
    return jnp.where(lane // per == row, 1.0, 0.0).astype(BF16)


def spread_heads(values, ones_rows):
    high, low = split_two(values)
    return dot_tn(jnp.concatenate([high, low], 0), jnp.concatenate([ones_rows, ones_rows], 0))


def sum_heads(values, ones_rows):
    high, low = split_two(values)
    return dot_nt(ones_rows, high) + dot_nt(ones_rows, low)


def window_before(ref, chunk, lanes):
    start = pl.multiple_of(chunk * CHUNK, CHUNK)
    before = pl.multiple_of(jnp.maximum(start - 8, 0), 8)
    halo = jnp.where(chunk > 0, ref[pl.ds(before, 8), lanes], 0.0)
    return jnp.concatenate([halo, ref[pl.ds(start, CHUNK), lanes]], 0)


def taps_of(window, tap_count):
    return [window[8:]] + [pltpu.roll(window, back, 0)[8:] for back in range(1, tap_count)]


def conv_of(shifted, table):
    last = len(shifted) - 1
    total = table[BIAS_ROW : BIAS_ROW + 1]
    for back, rows in enumerate(shifted):
        total = total + table[last - back : last - back + 1] * rows
    return total


def pair_blocks(pair):
    lane = lax.broadcasted_iota(jnp.int32, pair.shape, 1)
    half = pair.shape[1] // 2
    zero = jnp.zeros_like(pair)
    return jnp.concatenate([jnp.where(lane < half, pair, zero), jnp.where(lane < half, zero, pair)], 0)


def step_tables(dt_raw, dt_bias, a_neg):
    shifted = dt_raw + dt_bias
    steps = jnp.maximum(shifted, 0.0) + jnp.log1p(jnp.exp(-jnp.abs(shifted)))
    rates = steps * a_neg
    row = lax.broadcasted_iota(jnp.int32, (CHUNK, CHUNK), 0)
    col = lax.broadcasted_iota(jnp.int32, (CHUNK, CHUNK), 1)
    upper = jnp.where(row <= col, 1.0, 0.0).astype(F32)
    totals = lax.dot_general(
        rates, upper, (((1,), (0,)), ((), ())), precision=PRECISE, preferred_element_type=F32
    )
    return shifted, steps, totals * LOG2E


def prepare(c, bc_ref, dt_ref, sb_ref, small_ref, heads, bcs, gs, tcol, rvt, e1t, e2t, keep=None):
    rows = pl.ds(pl.multiple_of(c * CHUNK, CHUNK), CHUNK)
    for lanes in (slice(0, 128), slice(128, 256)):
        shifted = taps_of(window_before(bc_ref, c, lanes), BIAS_ROW)
        conv_out = conv_of(shifted, sb_ref[:, lanes])
        bcs[rows, lanes] = (conv_out * sigmoid(conv_out)).astype(BF16)
    b_rows = bcs[rows, 0:128]
    c_rows = bcs[rows, 128:256]
    gs[rows, :] = dot_nt(c_rows, b_rows)
    dt_raw = dt_ref[rows, :].T[:heads]
    shifted, steps, totals = step_tables(dt_raw, small_ref[:, 0:1], small_ref[:, 1:2])
    below = jnp.log2(steps) - totals
    pad = jnp.zeros((LANES - heads, CHUNK), F32)
    tcol[rows, :] = jnp.concatenate([totals, pad], 0).T
    rvt[c] = below
    e1t[c] = jnp.exp2(totals)
    e2t[c] = jnp.exp2(totals[:, CHUNK - 1 :] + below)
    if keep is not None:
        keep(c, shifted, steps)


def head_table(sh_ref, small_ref):
    row = lax.broadcasted_iota(jnp.int32, sh_ref.shape, 0)
    values = jnp.where(row == 1, -jnp.exp(sh_ref[...]), sh_ref[...])
    pad = jnp.zeros((LANES - sh_ref.shape[0], LANES), F32)
    small_ref[...] = jnp.concatenate([values, pad], 0).T[: small_ref.shape[0]]


def skip_of(small_ref, mine, ones_rows):
    return spread_heads(jnp.broadcast_to(small_ref[mine, 2:3], (GROUP, LANES)), ones_rows)[:1]


def decay_of(totals_col, below_row):
    row = lax.broadcasted_iota(jnp.int32, (CHUNK, CHUNK), 0)
    col = lax.broadcasted_iota(jnp.int32, (CHUNK, CHUNK), 1)
    return jnp.exp2(jnp.where(row >= col, totals_col + below_row, -jnp.inf))


def columns_of(tcol_chunk, group):
    shift = lax.rem(LANES - group * GROUP, LANES)
    return pltpu.roll(tcol_chunk, shift, 1)


def scan_forward(
    x_ref, bc_ref, dt_ref, sx_ref, sb_ref, sh_ref,
    mixed_ref, states_ref,
    bcs, gs, tcol, rvt, e1t, e2t, small_ref, state, xe2,
    *, heads,
):
    group = pl.program_id(1)
    chunks = x_ref.shape[0] // CHUNK
    width = x_ref.shape[1]
    ones_rows = head_rows(width, GROUP)

    @pl.when(group == 0)
    def _():
        head_table(sh_ref, small_ref)

        def one(c, carry):
            prepare(c, bc_ref, dt_ref, sb_ref, small_ref, heads, bcs, gs, tcol, rvt, e1t, e2t)
            return carry

        lax.fori_loop(0, chunks, one, 0)

    state[...] = jnp.zeros_like(state)
    mine = pl.ds(pl.multiple_of(group * GROUP, GROUP), GROUP)
    skip_row = skip_of(small_ref, mine, ones_rows)

    def chunk_step(c, carry):
        rows = pl.ds(pl.multiple_of(c * CHUNK, CHUNK), CHUNK)
        e1 = spread_heads(e1t[c, mine, :], ones_rows)
        e2 = spread_heads(e2t[c, mine, :], ones_rows)
        below = rvt[c, mine, :]
        columns = columns_of(tcol[rows, :], group)
        scores = gs[rows, :]
        state_now = state[...]
        state_b = state_now.astype(BF16)
        states_ref[0, c] = state_b
        carried = dot_nn(bcs[rows, 128:256], state_b) * e1
        for pair in range(width // LANES):
            lanes = slice(pair * LANES, (pair + 1) * LANES)
            shifted = taps_of(window_before(x_ref, c, lanes), BIAS_ROW)
            conv_out = conv_of(shifted, sx_ref[:, lanes])
            x = conv_out * sigmoid(conv_out)
            mixing = []
            for head in (2 * pair, 2 * pair + 1):
                decay = decay_of(columns[:, head : head + 1], below[head : head + 1])
                mixing.append((scores * decay).astype(BF16))
            local = dot_nn(jnp.concatenate(mixing, 1), pair_blocks(x.astype(BF16)))
            mixed_ref[rows, lanes] = local + carried[:, lanes] + skip_row[:, lanes] * x
            xe2[:, lanes] = (x * e2[:, lanes]).astype(BF16)
        state[...] = e1[CHUNK - 1 :] * state_now + dot_tn(bcs[rows, 0:128], xe2[...])
        return carry

    lax.fori_loop(0, chunks, chunk_step, 0)


def load_rows(sources, target, sem):
    copies = []
    for j, source in enumerate(sources):
        rows = source.shape[0]
        copies.append(pltpu.make_async_copy(source, target.at[pl.ds(j * rows, rows)], sem.at[j]))
    for copy in copies:
        copy.start()
    return copies


def load_lanes(sources, target, sem):
    copies = []
    for j, source in enumerate(sources):
        rows, wide = source.shape
        copies.append(pltpu.make_async_copy(source, target.at[pl.ds(0, rows), pl.ds(j * wide, wide)], sem.at[j]))
    for copy in copies:
        copy.start()
    if target.shape[0] > rows:
        target[rows:, :] = jnp.zeros((target.shape[0] - rows, target.shape[1]), target.dtype)
    return copies


def norm_kernel(n, order, info_ref, *refs):
    parts, (pre_ref, out_ref, turned_ref) = refs[:n], refs[n:]
    wide = parts[0].shape[1]
    values = [part[...].astype(F32) for part in parts]
    total = sum(jnp.sum(v * v, 1, keepdims=True) for v in values)
    scale = lax.rsqrt(total / (n * wide) + EPSILON)
    for j, v in enumerate(values):
        place = pl.ds(pl.multiple_of((info_ref[0] ^ order[j]) * wide, wide), wide)
        normed = (v * scale * pre_ref[PRE_ROW : PRE_ROW + 1, place]).astype(BF16)
        out_ref[:, j * wide : (j + 1) * wide] = normed
        turned_ref[j * wide : (j + 1) * wide, :] = normed.T


def project_kernel(n, normed_ref, *refs):
    blocks, (out_ref, weights, sem) = refs[:n], refs[n:]

    @pl.when(pl.program_id(0) == 0)
    def _():
        for copy in load_lanes(blocks, weights, sem):
            copy.wait()

    normed = normed_ref[...]
    wide = 512
    for start in range(0, out_ref.shape[1], wide):
        part = slice(start, min(start + wide, out_ref.shape[1]))
        out_ref[:, part] = dot_nt(normed, weights[part, :])


def gate_kernel(n, order, heads, seq_len, loads, info_ref, normed_ref, cot_ref, mixed_ref, gain_ref, *refs):
    wg_blocks, wo_blocks = refs[:loads], refs[loads : loads + n]
    nm_ref, turned_ref, dy_ref, gg_ref, gb_ref, r1_ref, gate, gnm, sig, wg, wo, sem_g, sem_o = refs[loads + n :]
    step = pl.program_id(0)
    rows = normed_ref.shape[0]
    inner = mixed_ref.shape[1]
    blocks = seq_len // rows
    me = info_ref[0]
    length = info_ref[2 + step // blocks]

    @pl.when(step == 0)
    def _():
        for copy in load_lanes(wg_blocks, wg, sem_g) + load_rows(wo_blocks, wo, sem_o):
            copy.wait()

    slot = lax.rem(step, blocks) * rows + lax.broadcasted_iota(jnp.int32, (rows, 1), 0)
    keep = slot < length
    cot_b = jnp.where(keep, cot_ref[...].astype(F32), 0.0).astype(BF16)
    gb_ref[...] = cot_b
    normed = normed_ref[...]
    squares = jnp.zeros((rows, LANES), F32)
    dots = jnp.zeros((rows, LANES), F32)
    wide = inner // n
    for j in range(n):
        block = slice(j * wide, (j + 1) * wide)
        place = pl.multiple_of((me ^ order[j]) * wide, wide)
        gate[:, block] = dot_nt(normed, wg[pl.ds(place, wide), :])
        gnm[:, block] = dot_nt(cot_b, wo[block, :])
        for lane in range(0, wide, LANES):
            lanes = slice(j * wide + lane, j * wide + lane + LANES)
            g = gate[:, lanes]
            s = sigmoid(g)
            sig[:, lanes] = s
            gated = mixed_ref[:, pl.ds(pl.multiple_of(place + lane, LANES), LANES)] * (g * s)
            squares = squares + gated * gated
            dots = dots + gnm[:, lanes] * gain_ref[GAIN_ROW : GAIN_ROW + 1, pl.ds(pl.multiple_of(place + lane, LANES), LANES)] * gated
    r = lax.rsqrt(jnp.sum(squares, 1, keepdims=True) / inner + EPSILON)
    mean = r * (jnp.sum(dots, 1, keepdims=True) / inner)
    r1 = jnp.zeros((heads, rows), F32)
    per = inner // heads
    for j in range(n):
        place = pl.multiple_of((me ^ order[j]) * wide, wide)
        for lane in range(0, wide, LANES):
            lanes = slice(j * wide + lane, j * wide + lane + LANES)
            spot = pl.multiple_of(place + lane, LANES)
            natural = pl.ds(spot, LANES)
            g = gate[:, lanes]
            s = sig[:, lanes]
            m = mixed_ref[:, natural]
            gain = gain_ref[GAIN_ROW : GAIN_ROW + 1, natural]
            up = gnm[:, lanes]
            silu = g * s
            unit = m * silu * r
            ggated = r * (up * gain - unit * mean)
            dy = (ggated * silu).astype(BF16)
            dy_ref[:, natural] = dy
            gg_ref[:, natural] = (ggated * m * (s + silu * (1.0 - s))).astype(BF16)
            nm = (unit * gain).astype(BF16)
            nm_ref[:, lanes] = nm
            turned_ref[lanes, :] = nm.T
            row = lax.broadcasted_iota(jnp.int32, (heads, LANES), 0)
            col = lax.broadcasted_iota(jnp.int32, (heads, LANES), 1) + spot
            ones_rows = jnp.where(col // per == row, 1.0, 0.0).astype(BF16)
            r1 = r1 + sum_heads(dy.astype(F32) * m, ones_rows)
    for k in range(rows // CHUNK):
        r1_ref[k] = r1[:, k * CHUNK : (k + 1) * CHUNK]


def branch_kernel(n, seq_len, info_ref, nm_ref, tok_ref, *refs):
    wo_blocks, (res_ref, wo, sem) = refs[:n], refs[n:]
    step = pl.program_id(0)
    rows = nm_ref.shape[0]
    blocks = seq_len // rows

    @pl.when(step == 0)
    def _():
        for copy in load_rows(wo_blocks, wo, sem):
            copy.wait()

    slot = lax.rem(step, blocks) * rows + lax.broadcasted_iota(jnp.int32, (rows, 1), 0)
    keep = slot < info_ref[2 + step // blocks]
    wide = min(512, wo.shape[1])
    for start in range(0, wo.shape[1], wide):
        part = slice(start, start + wide)
        branch = dot_nn(nm_ref[...], wo[:, part])
        res_ref[:, part] = jnp.where(keep, tok_ref[:, part].astype(F32) + branch, 0.0).astype(BF16)


def store_blocks(out_ref, values, base, sub):
    blocks, _, r, _ = out_ref.shape
    for b in range(blocks):
        for k in range(sub):
            rows = slice((base + b * sub + k) * r, (base + b * sub + k + 1) * r)
            for c in range(values.shape[1] // LANES):
                out_ref[b, c * sub + k] = values[rows, c * LANES : (c + 1) * LANES].astype(BF16)


def add_blocks(values, recv_ref, sub):
    blocks, _, _, _ = recv_ref.shape
    rows = []
    for b in range(blocks):
        for k in range(sub):
            lanes = [recv_ref[b, c * sub + k] for c in range(values.shape[1] // LANES)]
            rows.append(jnp.concatenate(lanes, 1))
    return values + jnp.concatenate(rows, 0).astype(F32)


def wgrad_kernel(plans, info_ref, *refs):
    refs = list(refs)
    take = lambda count: [refs.pop(0) for _ in range(count)]
    inputs = [take(1 + len(plan["cuts"]) + (plan["split"] is not None)) for plan in plans]
    outputs = [take(1 if plan["split"] is None else 2) for plan in plans]
    step = pl.program_id(0)

    def finish(plan, ins, outs, values, local):
        sub = plan["sub"]
        if plan["split"] is None:
            store_blocks(outs[0], values, 0, sub)
            return
        values = add_blocks(values, ins[-1], sub)
        kept_ref, sent_ref = outs
        if plan["split"] == "f":
            store_blocks(kept_ref, values, 0, sub)
            store_blocks(sent_ref, values, kept_ref.shape[0] * sub, sub)
        else:
            half = plan["steps"] // 2

            @pl.when(local < half)
            def _():
                store_blocks(kept_ref, values, 0, sub)

            @pl.when(local >= half)
            def _():
                store_blocks(sent_ref, values, 0, sub)

    for plan, ins, outs in zip(plans, inputs, outputs):
        local = step - plan["start"]
        low = 0
        for k, cut in enumerate(plan["cuts"]):

            @pl.when((local >= low) & (local < low + cut))
            def _(plan=plan, ins=ins, outs=outs, local=local, k=k):
                finish(plan, ins, outs, dot_nn(ins[0][...], ins[1 + k][...]), local)

            low += cut


def sum_kernel(plans, info_ref, *refs):
    total_in = sum(sum(sizes) for sizes in plans)
    inputs, outs = refs[:total_in], refs[total_in:]
    at = 0
    for sizes, out_ref in zip(plans, outs):
        base = 0
        for size in sizes:
            total = inputs[at][...].astype(F32)
            for ref in inputs[at + 1 : at + size]:
                total = total + ref[...].astype(F32)
            out_ref[:, base : base + total.shape[1]] = total.astype(BF16)
            base += total.shape[1]
            at += size


def assemble_kernel(plan, turn, info_ref, *refs):
    parts = refs[: 4 * len(plan)]
    weight_ref, out_ref, sums_ref, whole = refs[4 * len(plan) :]
    mine = (info_ref[1] & 1) * 2 + ((info_ref[1] >> 1) & 1)
    for p, (lane, blocks, first, sub) in enumerate(plan):
        for flip, ref in zip((0, 2, 1, 3), parts[4 * p : 4 * p + 4]):
            quarter = mine ^ flip
            r = ref.shape[2]
            for k in range(blocks):
                spot = pl.multiple_of(lane + (quarter * (blocks // sub) + k // sub) * LANES, LANES)
                block = ref[0, first + k].astype(F32)
                if turn:
                    whole[pl.ds(spot, LANES), :] = block.T
                else:
                    whole[slice((k % sub) * r, (k % sub + 1) * r), pl.ds(spot, LANES)] = block
    if turn:
        values = whole[: out_ref.shape[0], :]
        dots = jnp.sum(values * weight_ref[...].astype(F32), 0, keepdims=True)
    else:
        values = whole[:, : out_ref.shape[1]]
        dots = jnp.sum(values * weight_ref[...].astype(F32), 1, keepdims=True)
    out_ref[...] = values
    sums_ref[...] = jnp.broadcast_to(dots, sums_ref.shape)


def final_kernel(n, order, loads, info_ref, gg_ref, gx_ref, gy_ref, gb_ref, cot_ref, tok_ref, pre_ref, *refs):
    wg_blocks, wr_blocks = refs[:loads], refs[loads : 2 * loads]
    out_ref, wg, wr, grads, sem_g, sem_r = refs[2 * loads :]
    me = info_ref[0]

    @pl.when(pl.program_id(0) == 0)
    def _():
        for copy in load_lanes(wg_blocks, wg, sem_g) + load_lanes(wr_blocks, wr, sem_r):
            copy.wait()

    width = tok_ref.shape[1]
    inner = gg_ref.shape[1]
    part = gx_ref.shape[1]
    wide = width // n
    tokens = tok_ref[...].astype(F32)
    scale = lax.rsqrt(jnp.sum(tokens * tokens, 1, keepdims=True) / width + EPSILON)
    rows = tokens.shape[0]
    dots = jnp.zeros((rows, 1), F32)
    for j in range(n):
        block = slice(j * wide, (j + 1) * wide)
        place = pl.ds(pl.multiple_of((me ^ order[j]) * wide, wide), wide)
        total = dot_nn(gg_ref[...], wg[:, block]) + dot_nn(gx_ref[...], wr[:part, block])
        total = total + dot_nn(gy_ref[...], wr[part:inner, block])
        total = (total + dot_nn(gb_ref[:, : wr.shape[0] - inner], wr[inner:, block])) * pre_ref[PRE_ROW : PRE_ROW + 1, place]
        grads[:, block] = total
        dots = dots + jnp.sum(total * (tok_ref[:, place].astype(F32) * scale), 1, keepdims=True)
    mean = dots / width
    for j in range(n):
        block = slice(j * wide, (j + 1) * wide)
        place = pl.ds(pl.multiple_of((me ^ order[j]) * wide, wide), wide)
        unit = tok_ref[:, place].astype(F32) * scale
        grad = scale * (grads[:, block] - unit * mean)
        out_ref[:, place] = (cot_ref[:, place].astype(F32) + grad).astype(BF16)


def conv_back(grad, halo, conv_w):
    last = BIAS_ROW - 1
    window = jnp.concatenate([grad, halo], 0)
    total = conv_w[last : last + 1] * grad
    size = window.shape[0]
    for ahead in range(1, last + 1):
        total = total + conv_w[last - ahead : last - ahead + 1] * pltpu.roll(window, size - ahead, 0)[:CHUNK]
    return total


def add_tap_grads(out_ref, lanes, grad, shifted):
    last = len(shifted) - 1
    for back, rows in enumerate(shifted):
        tap = last - back
        out_ref[tap : tap + 1, lanes] += jnp.sum(grad * rows, 0, keepdims=True)
    out_ref[last + 1 : last + 2, lanes] += jnp.sum(grad, 0, keepdims=True)


def scan_backward(
    x_ref, bc_ref, dt_ref, dy_ref, states_ref, r1_ref, sx_ref, sb_ref, sh_ref, *refs, heads, first, last,
):
    refs = list(refs)
    take = lambda count: [refs.pop(0) for _ in range(count)]
    given = [] if first else take(7)
    gx_ref, convx_ref = take(2)
    if last:
        gbcdt_ref, convb_ref, heads_ref = take(3)
    sums_refs = take(7)
    tables = take(9)
    adj, xe2, hs, halo = take(4)
    seq = pl.program_id(1)
    step = pl.program_id(0)
    group = step + FIRST_OF[first]
    groups = pl.num_programs(0)
    chunks = x_ref.shape[0] // CHUNK
    width = x_ref.shape[1]
    ones_rows = head_rows(width, GROUP)
    bcs, gs, tcol, rvt, e1t, e2t, small_ref, shs, sts = [table.at[seq] for table in tables]
    dgs, dbs, dcs, colz, vsum, r2s, ends = [ref.at[seq] for ref in sums_refs]
    mine = pl.ds(pl.multiple_of(group * GROUP, GROUP), GROUP)

    @pl.when(step == 0)
    def _():
        head_table(sh_ref, small_ref)

        def keep(c, shifted, steps):
            shs[c] = shifted
            sts[c] = steps

        def one(c, carry):
            prepare(c, bc_ref, dt_ref, sb_ref, small_ref, heads, bcs, gs, tcol, rvt, e1t, e2t, keep)
            return carry

        lax.fori_loop(0, chunks, one, 0)
        if first:
            dgs[...] = jnp.zeros_like(dgs)
            dbs[...] = jnp.zeros_like(dbs)
            dcs[...] = jnp.zeros_like(dcs)
        else:
            for source, target in zip(given, (dgs, dbs, dcs, colz, vsum, r2s, ends)):
                target[...] = source[seq]

    skip_row = skip_of(small_ref, mine, ones_rows)
    adj[...] = jnp.zeros_like(adj)
    halo[...] = jnp.zeros_like(halo)

    @pl.when(seq == 0)
    def _():
        convx_ref[...] = jnp.zeros_like(convx_ref)

    def chunk_step(i, carry):
        c = chunks - 1 - i
        rows = pl.ds(pl.multiple_of(c * CHUNK, CHUNK), CHUNK)
        e1 = spread_heads(e1t[c, mine, :], ones_rows)
        e2 = spread_heads(e2t[c, mine, :], ones_rows)
        below = rvt[c, mine, :]
        columns = columns_of(tcol[rows, :], group)
        scores = gs[rows, :]
        adj_now = adj[...]
        adj_b = adj_now.astype(BF16)
        state_b = states_ref[0, c]
        b_rows = bcs[rows, 0:128]
        c_rows = bcs[rows, 128:256]
        from_adj = dot_nn(b_rows, adj_b) * e2
        cross = e1[CHUNK - 1 :] * jnp.sum(adj_now * state_b.astype(F32), 0, keepdims=True)
        dg = dgs[rows, :]
        col_total = jnp.zeros((GROUP, CHUNK), F32)
        v_total = jnp.zeros((GROUP, CHUNK), F32)
        r2_total = jnp.zeros((GROUP, CHUNK), F32)
        for pair in range(width // LANES):
            lanes = slice(pair * LANES, (pair + 1) * LANES)
            shifted = taps_of(window_before(x_ref, c, lanes), BIAS_ROW)
            conv_out = conv_of(shifted, sx_ref[:, lanes])
            s = sigmoid(conv_out)
            x = conv_out * s
            xb = x.astype(BF16)
            dyb = dy_ref[rows, lanes]
            dy = dyb.astype(F32)
            both = dot_nt(dyb, pair_blocks(xb))
            mixing = []
            for k, head in enumerate((2 * pair, 2 * pair + 1)):
                decay = decay_of(columns[:, head : head + 1], below[head : head + 1])
                mixing.append((scores * decay).astype(BF16))
                dg = dg + both[:, k * CHUNK : (k + 1) * CHUNK] * decay
            local = dot_tn(jnp.concatenate(mixing, 0), pair_blocks(dyb))
            tail = from_adj[:, lanes]
            dx = local + tail + skip_row[:, lanes] * dy
            grad = dx * (s + x * (1.0 - s))
            gx_ref[rows, lanes] = conv_back(grad, halo[:, lanes], sx_ref[:, lanes]).astype(BF16)
            halo[:, lanes] = grad[:8]
            add_tap_grads(convx_ref, lanes, grad, shifted)
            hs[:, lanes] = (dy * e1[:, lanes]).astype(BF16)
            xe2[:, lanes] = (x * e2[:, lanes]).astype(BF16)
            pair_ones = ones_rows[:, lanes]
            col_total = col_total + sum_heads(xb.astype(F32) * local, pair_ones)
            v_total = v_total + sum_heads(x * tail, pair_ones)
            r2_total = r2_total + sum_heads(dy * x, pair_ones)
        dgs[rows, :] = dg
        colz[c, mine, :] = col_total
        vsum[c, mine, :] = v_total
        r2s[c, mine, :] = r2_total
        ends[c, mine, :] = jnp.broadcast_to(
            sum_heads(jnp.broadcast_to(cross, (8, width)), ones_rows)[:, 0:1], (GROUP, CHUNK)
        )
        dcs[rows, :] += dot_nt(hs[...], state_b)
        dbs[rows, :] += dot_nt(xe2[...], adj_b)
        adj[...] = e1[CHUNK - 1 :] * adj_now + dot_tn(c_rows, hs[...])
        return carry

    lax.fori_loop(0, chunks, chunk_step, 0)
    if not last:
        return

    @pl.when(step == groups - 1)
    def _():
        @pl.when(seq == 0)
        def _():
            convb_ref[...] = jnp.zeros_like(convb_ref)
            heads_ref[...] = jnp.zeros_like(heads_ref)

        halo[...] = jnp.zeros_like(halo)
        row = lax.broadcasted_iota(jnp.int32, (CHUNK, CHUNK), 0)
        col = lax.broadcasted_iota(jnp.int32, (CHUNK, CHUNK), 1)
        later = jnp.where(row >= col, 1.0, 0.0).astype(F32)
        earlier = jnp.where(row < col, 1.0, 0.0).astype(F32)
        a_neg = small_ref[:, 1:2]
        skip = small_ref[:, 2:3]

        def finish(i, carry):
            bias_sum, log_sum, skip_sum = carry
            c = chunks - 1 - i
            rows = pl.ds(pl.multiple_of(c * CHUNK, CHUNK), CHUNK)
            dg = dgs[rows, :].astype(BF16)
            b_rows = bcs[rows, 0:128]
            c_rows = bcs[rows, 128:256]
            totals = (dbs[rows, :] + dot_tn(dg, c_rows), dcs[rows, :] + dot_nn(dg, b_rows))
            for lanes, total in zip((slice(0, 128), slice(128, 256)), totals):
                shifted = taps_of(window_before(bc_ref, c, lanes), BIAS_ROW)
                conv_out = conv_of(shifted, sb_ref[:, lanes])
                s = sigmoid(conv_out)
                grad = total * (s + conv_out * s * (1.0 - s))
                gbcdt_ref[rows, lanes] = conv_back(grad, halo[:, lanes], sb_ref[:, lanes]).astype(BF16)
                halo[:, lanes] = grad[:8]
                add_tap_grads(convb_ref, lanes, grad, shifted)
            inner_part = r1_ref[c] - skip * r2s[c] - colz[c]
            dims = (((1,), (0,)), ((), ()))
            q = (
                lax.dot_general(inner_part, later, dims, precision=PRECISE, preferred_element_type=F32)
                + lax.dot_general(vsum[c], earlier, dims, precision=PRECISE, preferred_element_type=F32)
                + ends[c]
            )
            shifted_dt = shs[c]
            steps = sts[c]
            sig = sigmoid(shifted_dt)
            ratio = jnp.where(shifted_dt < -15.0, 1.0, sig / steps)
            grad_dt = ratio * (colz[c] + vsum[c]) + sig * a_neg * q
            pad = jnp.zeros((LANES - heads, CHUNK), F32)
            gbcdt_ref[rows, 256:384] = jnp.concatenate([grad_dt, pad], 0).T.astype(BF16)
            gbcdt_ref[rows, 384:512] = jnp.zeros((CHUNK, LANES), BF16)
            total_of = lambda v: jnp.sum(v, 1, keepdims=True)
            return (
                bias_sum + total_of(grad_dt), log_sum + a_neg * total_of(steps * q), skip_sum + total_of(r2s[c])
            )

        zero = jnp.zeros((heads, 1), F32)
        columns = jnp.concatenate(lax.fori_loop(0, chunks, finish, (zero, zero, zero)), 1)
        columns = jnp.pad(columns, ((0, LANES - heads), (0, LANES - 3)))
        heads_ref[...] += columns.T[:8]


def cost(us):
    return pl.CostEstimate(flops=int(us * 1e9), bytes_accessed=int(us * 1e5), transcendentals=0)


def params():
    return pltpu.CompilerParams(vmem_limit_bytes=VMEM_BYTES)


def scan_specs(seq_len, width, inner):
    return dict(
        x=pl.BlockSpec((seq_len, width), lambda m, g: (m, g)),
        bc=pl.BlockSpec((seq_len, 256), lambda m, g: (m, inner // 256)),
        dt=pl.BlockSpec((seq_len, LANES), lambda m, g: (m, inner // LANES + 2)),
        sx=pl.BlockSpec((8, width), lambda m, g: (0, g)),
        sb=pl.BlockSpec((8, 256), lambda m, g: (0, inner // 256)),
        sh=pl.BlockSpec((8, LANES), lambda m, g: (0, inner // LANES + 2)),
    )


def table_scratch(seq_len, heads):
    chunks = seq_len // CHUNK
    return [
        pltpu.VMEM((seq_len, 256), BF16),
        pltpu.VMEM((seq_len, CHUNK), F32),
        pltpu.VMEM((seq_len, LANES), F32),
        pltpu.VMEM((chunks, heads, CHUNK), F32),
        pltpu.VMEM((chunks, heads, CHUNK), F32),
        pltpu.VMEM((chunks, heads, CHUNK), F32),
        pltpu.VMEM((heads, LANES), F32),
    ]


def call_forward(rest, smalls, seq_count, inner, heads):
    seq_len = rest.shape[0] // seq_count
    width = GROUP * (inner // heads)
    chunks = seq_len // CHUNK
    sp = scan_specs(seq_len, width, inner)
    return pl.pallas_call(
        functools.partial(scan_forward, heads=heads),
        grid=(seq_count, inner // width),
        in_specs=[sp["x"], sp["bc"], sp["dt"], sp["sx"], sp["sb"], sp["sh"]],
        out_specs=[pl.BlockSpec((seq_len, width), lambda m, g: (m, g)),
                   pl.BlockSpec((1, chunks, 128, width), lambda m, g: (m, 0, 0, g))],
        out_shape=[jax.ShapeDtypeStruct((rest.shape[0], inner), F32),
                   jax.ShapeDtypeStruct((seq_count, chunks, 128, inner), BF16)],
        scratch_shapes=table_scratch(seq_len, heads) + [
            pltpu.VMEM((128, width), F32),
            pltpu.VMEM((CHUNK, width), BF16),
        ],
        compiler_params=params(),
        cost_estimate=cost(25),
        name="scan_forward",
    )(rest, rest, rest, smalls, smalls, smalls)


def in_hbm(count):
    return [pl.BlockSpec(memory_space=pl.ANY)] * count


def call_norm(info, tokens, smalls, n, order):
    total, width = tokens.shape
    rows = 2 * CHUNK
    wide = width // n
    spec = lambda j: pl.BlockSpec((rows, wide), lambda i, info: (i, info[0] ^ order[j]))
    return pl.pallas_call(
        functools.partial(norm_kernel, n, order),
        grid_spec=pltpu.PrefetchScalarGridSpec(
            num_scalar_prefetch=1,
            grid=(total // rows,),
            in_specs=[spec(j) for j in range(n)] + [pl.BlockSpec(smalls.shape, lambda i, _: (0, 0))],
            out_specs=[pl.BlockSpec((rows, width), lambda i, _: (i, 0)),
                       pl.BlockSpec((width, rows), lambda i, _: (0, i))],
        ),
        out_shape=[jax.ShapeDtypeStruct((total, width), BF16), jax.ShapeDtypeStruct((width, total), BF16)],
        compiler_params=params(),
        cost_estimate=cost(4),
        name="norm",
    )(info, *([tokens] * n), smalls)


def call_project(normed, blocks):
    total, width = normed.shape
    rows = 2 * CHUNK
    cols = blocks[0].shape[0]
    cols += -cols % LANES
    n = len(blocks)
    return pl.pallas_call(
        functools.partial(project_kernel, n),
        grid=(total // rows,),
        in_specs=[pl.BlockSpec((rows, width), lambda i: (i, 0))] + in_hbm(n),
        out_specs=pl.BlockSpec((rows, cols), lambda i: (i, 0)),
        out_shape=jax.ShapeDtypeStruct((total, cols), F32),
        scratch_shapes=[pltpu.VMEM((cols, width), BF16), pltpu.SemaphoreType.DMA((n,))],
        compiler_params=params(),
        cost_estimate=cost(11),
        name="project",
    )(normed, *blocks)


def call_gate(info, normed, cot, mixed, smalls, gate_blocks, out_blocks, order, heads, seq_len):
    total, width = normed.shape
    inner = mixed.shape[1]
    rows = GATE_ROWS
    steps = total // rows
    n, loads = len(out_blocks), len(gate_blocks)
    blk = lambda w: pl.BlockSpec((rows, w), lambda i, _: (i, 0))
    return pl.pallas_call(
        functools.partial(gate_kernel, n, order, heads, seq_len, loads),
        grid_spec=pltpu.PrefetchScalarGridSpec(
            num_scalar_prefetch=1,
            grid=(steps,),
            in_specs=[blk(width), blk(width), blk(inner), pl.BlockSpec(smalls.shape, lambda i, _: (0, 0))]
            + in_hbm(loads + n),
            out_specs=[blk(inner), pl.BlockSpec((inner, rows), lambda i, _: (0, i)), blk(inner), blk(inner), blk(width),
                       pl.BlockSpec((rows // CHUNK, heads, CHUNK), lambda i, _: (i, 0, 0))],
            scratch_shapes=[pltpu.VMEM((rows, inner), F32)] * 3 + [
                pltpu.VMEM((inner, width), BF16), pltpu.VMEM((inner, width), BF16),
                pltpu.SemaphoreType.DMA((loads,)), pltpu.SemaphoreType.DMA((n,))],
        ),
        out_shape=[jax.ShapeDtypeStruct((total, inner), BF16), jax.ShapeDtypeStruct((inner, total), BF16)] + [
            jax.ShapeDtypeStruct((total, inner), BF16)] * 2 + [
            jax.ShapeDtypeStruct((total, width), BF16),
            jax.ShapeDtypeStruct((total // CHUNK, heads, CHUNK), F32)],
        compiler_params=params(),
        cost_estimate=cost(30),
        name="gate",
    )(info, normed, cot, mixed, smalls, *gate_blocks, *out_blocks)


def call_branch(info, nm, tokens, out_blocks, seq_len):
    total, inner = nm.shape
    width = tokens.shape[1]
    rows = 2 * CHUNK
    n = len(out_blocks)
    blk = lambda w: pl.BlockSpec((rows, w), lambda i, _: (i, 0))
    return pl.pallas_call(
        functools.partial(branch_kernel, n, seq_len),
        grid_spec=pltpu.PrefetchScalarGridSpec(
            num_scalar_prefetch=1,
            grid=(total // rows,),
            in_specs=[blk(inner), blk(width)] + in_hbm(n),
            out_specs=blk(width),
            scratch_shapes=[pltpu.VMEM((inner, width), BF16), pltpu.SemaphoreType.DMA((n,))],
        ),
        out_shape=jax.ShapeDtypeStruct((total, width), BF16),
        compiler_params=params(),
        cost_estimate=cost(9),
        name="branch",
    )(info, nm, tokens, *out_blocks)


def call_wgrad(info, jobs, n, r, side, us=8):
    blocks = n // 2
    plans, specs, args, out_specs, out_shape = [], [], [], [], []
    start = 0
    for left, rights, recv, split in jobs:
        rows, slots = left.shape
        half = rows // 2
        sub = half // (blocks * r)
        cuts = [right.shape[1] // WIDE for right in rights]
        steps = sum(cuts)
        plans.append(dict(cuts=cuts, start=start, steps=steps, sub=sub, split=split))

        def local_of(i, start=start, steps=steps):
            return jnp.clip(i - start, 0, steps - 1)

        def chunk_of(i, info, local_of=local_of, steps=steps, split=split):
            if split == "r":
                return lax.rem(local_of(i) + (info[1] & 1) * (steps // 2), steps)
            return local_of(i)

        block = lambda b: (b, WIDE // LANES * sub, r, LANES)
        shape = lambda b, c: jax.ShapeDtypeStruct((b, c, r, LANES), BF16)
        count = steps * (WIDE // LANES) * sub
        specs.append(pl.BlockSpec((half, slots), lambda i, info: (side, 0)))
        args.append(left)
        low = 0
        for right, cut in zip(rights, cuts):
            specs.append(pl.BlockSpec((slots, WIDE), functools.partial(
                lambda chunk_of, low, cut, i, info: (0, jnp.clip(chunk_of(i, info) - low, 0, cut - 1)),
                chunk_of, low, cut)))
            args.append(right)
            low += cut
        if split is None:
            out_specs.append(pl.BlockSpec(block(blocks), functools.partial(
                lambda local_of, i, info: (0, local_of(i), 0, 0), local_of)))
            out_shape.append(shape(blocks, count))
        else:
            specs.append(pl.BlockSpec(block(blocks), functools.partial(
                lambda chunk_of, i, info: (0, chunk_of(i, info), 0, 0), chunk_of)))
            args.append(recv)
            if split == "f":
                out_specs += [pl.BlockSpec(block(blocks // 2), functools.partial(
                    lambda local_of, i, info: (0, local_of(i), 0, 0), local_of))] * 2
                out_shape += [shape(blocks // 2, count)] * 2
            else:
                mid = steps // 2
                out_specs += [
                    pl.BlockSpec(block(blocks), functools.partial(
                        lambda local_of, mid, i, info: (0, jnp.minimum(local_of(i), mid - 1), 0, 0), local_of, mid)),
                    pl.BlockSpec(block(blocks), functools.partial(
                        lambda local_of, mid, i, info: (0, jnp.maximum(local_of(i) - mid, 0), 0, 0), local_of, mid))]
                out_shape += [shape(blocks, count // 2)] * 2
        start += steps
    return pl.pallas_call(
        functools.partial(wgrad_kernel, plans),
        grid_spec=pltpu.PrefetchScalarGridSpec(
            num_scalar_prefetch=1, grid=(start,), in_specs=specs, out_specs=out_specs),
        out_shape=out_shape,
        compiler_params=params(),
        cost_estimate=cost(us),
        name="wgrad",
    )(info, *args)


def call_sums(info, *jobs):
    specs, args, out_specs, out_shape, plans = [], [], [], [], []
    for groups, axis, count, picks in jobs:
        for pick in picks:
            width = 0
            for group in groups:
                for value in group:
                    shape = list(value.shape)
                    shape[axis] //= count
                    place = functools.partial(lambda pick, axis, i, info: tuple(
                        pick(info[1]) if k == axis else 0 for k in range(4)), pick, axis)
                    specs.append(pl.BlockSpec(tuple(shape), place))
                    args.append(value)
                width += shape[1]
            out = (shape[0], width) + tuple(shape[2:])
            out_specs.append(pl.BlockSpec(out, lambda i, info: (0, 0, 0, 0)))
            out_shape.append(jax.ShapeDtypeStruct(out, BF16))
            plans.append([len(group) for group in groups])
    return pl.pallas_call(
        functools.partial(sum_kernel, plans),
        grid_spec=pltpu.PrefetchScalarGridSpec(
            num_scalar_prefetch=1, grid=(1,), in_specs=specs, out_specs=out_specs),
        out_shape=out_shape,
        compiler_params=params(),
        cost_estimate=cost(3),
        name="sum",
    )(info, *args)


def call_assemble(info, pieces, plan, weight, turn):
    parts = [part for piece in pieces for part in piece]
    wide = max(lane + 4 * (blocks // sub) * LANES for lane, blocks, first, sub in plan)
    if turn:
        cols, rows = weight.shape
        step = min(rows, LANES)
        steps = rows // step
        big = pl.BlockSpec((cols, step), lambda i, _: (0, i))
        line = pl.BlockSpec((8, step), lambda i, _: (0, i))
        sums, scratch = (8, rows), (wide, step)
    else:
        rows, cols = weight.shape
        step, steps = parts[0].shape[2], 1
        big = pl.BlockSpec((rows, cols), lambda i, _: (0, 0))
        line = pl.BlockSpec((rows, LANES), lambda i, _: (0, 0))
        sums, scratch = (rows, LANES), (rows, wide)
    part_spec = lambda p: pl.BlockSpec(p.shape[:2] + (step, LANES), lambda i, _: (0, 0, i, 0))
    return pl.pallas_call(
        functools.partial(assemble_kernel, plan, turn),
        grid_spec=pltpu.PrefetchScalarGridSpec(
            num_scalar_prefetch=1,
            grid=(steps,),
            in_specs=[part_spec(part) for part in parts] + [big],
            out_specs=[big, line],
            scratch_shapes=[pltpu.VMEM(scratch, F32)],
        ),
        out_shape=[jax.ShapeDtypeStruct(weight.shape, F32), jax.ShapeDtypeStruct(sums, F32)],
        compiler_params=params(),
        cost_estimate=cost(4),
        name="assemble",
    )(info, *parts, weight)


def call_final(info, gg, gx, gy, gbcdt, gb, tokens, smalls, gate_blocks, rest_blocks, n, order):
    total, width = tokens.shape
    inner = gg.shape[1]
    rows = 2 * CHUNK
    loads = len(gate_blocks)
    blk = lambda w: pl.BlockSpec((rows, w), lambda i, _: (i, 0))
    cols = rest_blocks[0].shape[0]
    cols += -cols % LANES
    return pl.pallas_call(
        functools.partial(final_kernel, n, order, loads),
        grid_spec=pltpu.PrefetchScalarGridSpec(
            num_scalar_prefetch=1,
            grid=(total // rows,),
            in_specs=[blk(inner), blk(gx.shape[1]), blk(gy.shape[1]), blk(gbcdt.shape[1]), blk(width), blk(width),
                      pl.BlockSpec(smalls.shape, lambda i, _: (0, 0))] + in_hbm(2 * loads),
            out_specs=blk(width),
            scratch_shapes=[pltpu.VMEM((inner, width), BF16), pltpu.VMEM((cols, width), BF16),
                            pltpu.VMEM((rows, width), F32),
                            pltpu.SemaphoreType.DMA((loads,)), pltpu.SemaphoreType.DMA((loads,))],
        ),
        out_shape=jax.ShapeDtypeStruct((total, width), BF16),
        compiler_params=params(),
        cost_estimate=cost(19),
        name="final",
    )(info, gg, gx, gy, gbcdt, gb, tokens, smalls, *gate_blocks, *rest_blocks)


def call_backward(rest, dy, states, r1, smalls, seq_count, inner, heads, sums=None):
    seq_len = rest.shape[0] // seq_count
    width = GROUP * (inner // heads)
    chunks = seq_len // CHUNK
    groups = inner // width
    first, last = sums is None, sums is not None
    base = 0 if first else SPLIT
    count = SPLIT if first else groups - SPLIT
    at = lambda g: g + base
    whole = lambda *shape: pl.BlockSpec(shape, lambda g, m: (0,) * len(shape))
    sum_shapes = [(seq_count, seq_len, CHUNK)] + [(seq_count, seq_len, 128)] * 2 + [
        (seq_count, chunks, heads, CHUNK)] * 4
    end = lambda g, m: jnp.where(g == count - 1, m, 0)
    out_specs = [pl.BlockSpec((seq_len, width), lambda g, m: (m, g)), pl.BlockSpec((8, width), lambda g, m: (0, g))]
    out_shape = [jax.ShapeDtypeStruct((rest.shape[0], count * width), BF16),
                 jax.ShapeDtypeStruct((8, count * width), F32)]
    scratch = []
    if last:
        out_specs += [pl.BlockSpec((seq_len, 512), lambda g, m: (end(g, m), 0)), whole(8, 256), whole(8, LANES)]
        out_shape += [jax.ShapeDtypeStruct((rest.shape[0], 512), BF16), jax.ShapeDtypeStruct((8, 256), F32),
                      jax.ShapeDtypeStruct((8, LANES), F32)]
        scratch = [pltpu.VMEM(shape, F32) for shape in sum_shapes]
    else:
        out_specs += [whole(*shape) for shape in sum_shapes]
        out_shape += [jax.ShapeDtypeStruct(shape, F32) for shape in sum_shapes]
    per_seq = lambda memory: pltpu.VMEM((seq_count,) + memory.shape, memory.dtype)
    tables = table_scratch(seq_len, heads) + [pltpu.VMEM((chunks, heads, CHUNK), F32)] * 2
    return pl.pallas_call(
        functools.partial(scan_backward, heads=heads, first=first, last=last),
        grid=(count, seq_count),
        in_specs=[pl.BlockSpec((seq_len, width), lambda g, m: (m, at(g))),
                  pl.BlockSpec((seq_len, 256), lambda g, m: (m, inner // 256)),
                  pl.BlockSpec((seq_len, LANES), lambda g, m: (m, inner // LANES + 2)),
                  pl.BlockSpec((seq_len, width), lambda g, m: (m, at(g))),
                  pl.BlockSpec((1, chunks, 128, width), lambda g, m: (m, 0, 0, at(g))),
                  pl.BlockSpec((chunks, heads, CHUNK), lambda g, m: (m, 0, 0)),
                  pl.BlockSpec((8, width), lambda g, m: (0, at(g))),
                  pl.BlockSpec((8, 256), lambda g, m: (0, inner // 256)),
                  pl.BlockSpec((8, LANES), lambda g, m: (0, inner // LANES + 2))]
        + ([] if first else [whole(*shape) for shape in sum_shapes]),
        out_specs=out_specs,
        out_shape=out_shape,
        scratch_shapes=scratch + [per_seq(memory) for memory in tables] + [
            pltpu.VMEM((128, width), F32),
            pltpu.VMEM((CHUNK, width), BF16),
            pltpu.VMEM((CHUNK, width), BF16),
            pltpu.VMEM((8, width), F32),
        ],
        compiler_params=params(),
        cost_estimate=cost(28),
        name="scan_backward",
    )(rest, rest, rest, dy, states, r1, smalls, smalls, smalls, *([] if first else sums))


def block_order(n):
    order = [0]
    mask = n // 2
    while mask:
        order = order + [o ^ mask for o in order]
        mask //= 2
    return order


def masks_of(n):
    return [1 << k for k in range(n.bit_length() - 1)]


def swap(value, axis, mask):
    n = lax.axis_size(axis)
    return lax.ppermute(value, axis, [(i, i ^ mask) for i in range(n)])


def y_bit(rep):
    return rep & 1


def z_bit(rep):
    return (rep >> 1) & 1


def quarter_of(rep):
    return y_bit(rep) * 2 + z_bit(rep)


HALF_Y = (y_bit, lambda rep: 1 - y_bit(rep))
HALF_Z = (z_bit, lambda rep: 1 - z_bit(rep))
FIRST = (lambda rep: 0, lambda rep: 1)
QUARTERS = (quarter_of, lambda rep: quarter_of(rep) ^ 2, lambda rep: quarter_of(rep) ^ 1, lambda rep: quarter_of(rep) ^ 3)


def all_of(*arrays):
    return ([list(group) for group in arrays], 0, 1, FIRST[:1])


def swap_far(info, total):
    for mask in masks_of(lax.axis_size("rep"))[3:]:
        (total,) = call_sums(info, all_of([total, swap(total, "rep", mask)]))
    return total


def gather_quarters(total):
    return [total] + [swap(total, "rep", mask) for mask in (1, 2, 3)]


def swap_all(own):
    held = [own]
    for mask in reversed(masks_of(lax.axis_size("fsdp"))[1:]):
        held = held + [swap(block, "fsdp", mask) for block in held]
    return held


def swap_cores(held):
    return held + [swap(block, "fsdp", 1) for block in held]


def share_small(pre_gain, conv_w, conv_b, dt_bias, a_log, d_skip, norm_gain):
    n = lax.axis_size("fsdp")
    me = lax.axis_index("fsdp")

    def line(part):
        part = part.reshape(-1, part.shape[-1])
        lane = lax.broadcasted_iota(jnp.int32, (part.shape[0], n * part.shape[1]), 1)
        return jnp.where(lane // part.shape[1] == me, jnp.concatenate([part] * n, 1), jnp.zeros((), part.dtype))

    conv = line(jnp.concatenate([conv_w, conv_b[None]], 0))
    pre, gain = line(pre_gain), line(norm_gain)
    head = line(jnp.stack([dt_bias, a_log, d_skip]))
    wide = conv.shape[1]
    fit = lambda v: jnp.pad(v, ((0, 0), (0, wide - v.shape[1])))
    left = jnp.concatenate([conv, fit(pre), fit(gain), jnp.zeros((1, wide), conv.dtype)], 0)
    whole = jnp.concatenate([left, jnp.pad(head, ((0, 5), (0, LANES - head.shape[1])))], 1)
    for mask in reversed(masks_of(n)):
        whole = whole + swap(whole, "fsdp", mask)
    return whole.astype(F32)


def in_blocks(value, order, me):
    n = len(order)
    parts = value.reshape(value.shape[0], n, -1)
    return jnp.take(parts, jnp.array(order) ^ me, axis=1).reshape(value.shape)


def on_device(
    inputs, cotangent, lengths, pre_gain, w_in, conv_w, conv_b, dt_bias, a_log, d_skip, norm_gain, w_out
):
    micro, seqs, seq_len, width = inputs.shape
    seq_count = micro * seqs
    rows = seq_count * seq_len
    n = lax.axis_size("fsdp")
    order = block_order(n)
    me = lax.axis_index("fsdp")
    inner = norm_gain.shape[0] * n
    heads = dt_bias.shape[0] * n
    taps, chans = conv_w.shape
    r = width // n
    weights_t = w_in.T
    own_rest = weights_t[inner:]
    tokens = inputs.reshape(rows, width)
    cot = cotangent.reshape(rows, width)
    info = jnp.concatenate([jnp.stack([me, lax.axis_index("rep")]).astype(jnp.int32), lengths.reshape(seq_count)])
    rest_x = swap_all(own_rest)
    smalls = share_small(pre_gain, conv_w, conv_b, dt_bias, a_log, d_skip, norm_gain)
    own_out = w_out
    own_gate, rest_x = lax.optimization_barrier((weights_t[:inner], rest_x))
    rest_blocks = swap_cores(rest_x)
    gate_x = swap_all(own_gate)
    gate_blocks = swap_cores(gate_x)
    aligned = r % LANES == 0
    if aligned:
        turn = lambda value: value
        side = lambda blocks: blocks
        parts, places, info_d, smalls_d = n, order, info, smalls
    else:
        turn = lambda value: in_blocks(value, order, me)
        side = lambda blocks: [jnp.concatenate(blocks, 1)]
        parts, places, info_d = 1, [0], info.at[0].set(0)
        smalls_d = jnp.concatenate([turn(smalls[:, :width]), smalls[:, width:]], 1)
    normed, normed_t = call_norm(info_d, turn(tokens), smalls_d, parts, places)
    rest_blocks, gate_blocks = side(rest_blocks), side(gate_blocks)
    rest = call_project(normed, rest_blocks)
    rest, own_out = lax.optimization_barrier((rest, own_out))
    out_x = swap_all(own_out)
    out_blocks = swap_cores(out_x)
    mixed, states = call_forward(rest, smalls, seq_count, inner, heads)
    nm, nm_t, dy, gg, gb, r1 = call_gate(
        info, normed, cot, mixed, smalls, gate_blocks, out_blocks, order, heads, seq_len
    )
    groups = masks_of(n)[1:]

    far = masks_of(lax.axis_size("rep"))[2]

    def shards_first(total, other):
        for mask in groups[1:]:
            total, sent = call_sums(info, ([[total, other]], 0, 2, FIRST))
            other = swap(sent, "fsdp", mask)
        return total, other

    out_send, gate_send = call_wgrad(info, [(nm_t, [gb], None, None), (normed_t, [gg], None, None)], n, r, 1)
    out_recv = swap(out_send, "fsdp", 1)
    gate_recv = swap(gate_send, "fsdp", 1)
    out_kept, out_send, gate_kept, gate_send = call_wgrad(
        info, [(nm_t, [gb], out_recv, "f"), (normed_t, [gg], gate_recv, "r")], n, r, 0)
    out_recv = swap(out_send, "fsdp", groups[0])
    gate_recv = swap(gate_send, "rep", 1)
    back = (rest, dy, states, r1, smalls, seq_count, inner, heads)
    gx_one, convx_one, *sums = call_backward(*back)
    (one_send,) = call_wgrad(info, [(normed_t, [gx_one], None, None)], n, r, 1, 4)
    one_recv = swap(one_send, "fsdp", 1)
    out_kept, out_recv = shards_first(out_kept, out_recv)
    out_kept, out_send, gate_kept, gate_send = call_sums(
        info, ([[out_kept, out_recv]], 1, 2, HALF_Y), ([[gate_kept, gate_recv]], 0, 2, FIRST))
    out_recv = swap(out_send, "rep", 1)
    gate_recv = swap(gate_send, "fsdp", groups[0])
    one_kept, one_send = call_wgrad(info, [(normed_t, [gx_one], one_recv, "f")], n, r, 0, 4)
    one_recv = swap(one_send, "fsdp", groups[0])
    gx_two, convx_two, gbcdt, convb, headg = call_backward(*back, sums)
    small_g = jnp.concatenate([convx_one, convx_two, convb, headg], 1)
    (two_send,) = call_wgrad(info, [(normed_t, [gx_two, gbcdt], None, None)], n, r, 1, 4)
    two_recv = swap(two_send, "fsdp", 1)
    gate_kept, gate_recv = shards_first(gate_kept, gate_recv)
    one_kept, one_recv = shards_first(one_kept, one_recv)
    wide_kept, wide_send, one_kept, one_send = call_sums(
        info, ([[out_kept, out_recv], [gate_kept, gate_recv]], 1, 2, HALF_Z), ([[one_kept, one_recv]], 1, 2, HALF_Y))
    wide_recv = swap(wide_send, "rep", 2)
    one_recv = swap(one_send, "rep", 1)
    two_kept, two_send = call_wgrad(info, [(normed_t, [gx_two, gbcdt], two_recv, "f")], n, r, 0, 4)
    two_recv = swap(two_send, "fsdp", groups[0])
    small_r = swap(small_g, "fsdp", 1)
    grad_in = call_final(
        info_d, gg, gx_one, gx_two, gbcdt, turn(gb), turn(tokens), smalls_d, gate_blocks, rest_blocks, parts, places
    )
    grad_in = turn(grad_in)
    small_g = small_g + small_r
    small_r = swap(small_g, "fsdp", groups[0])
    two_kept, two_recv = shards_first(two_kept, two_recv)
    wide, one_kept, one_send, two_kept, *two_sends = call_sums(
        info, all_of([wide_kept, wide_recv]), ([[one_kept, one_recv]], 1, 2, HALF_Z),
        ([[two_kept, two_recv]], 1, 4, QUARTERS))
    wide_recv = swap(wide, "rep", far)
    one_recv = swap(one_send, "rep", 2)
    two_recvs = [swap(sent, "rep", mask) for mask, sent in zip((1, 2, 3), two_sends)]
    res = call_branch(info, nm, tokens, out_blocks, seq_len)
    small_g = small_g + small_r
    for mask in groups[1:]:
        small_g = small_g + swap(small_g, "fsdp", mask)
    small_r = swap(small_g, "rep", 1)
    wide, one, two = call_sums(
        info, all_of([wide, wide_recv]), all_of([one_kept, one_recv]), all_of([two_kept] + two_recvs))
    one_recv = swap(one, "rep", far)
    two_recv = swap(two, "rep", far)
    wide = gather_quarters(swap_far(info, wide))
    small_r, one = lax.optimization_barrier((small_r, one))
    small_g = small_g + small_r
    small_r = swap(small_g, "rep", 2)
    one, two = call_sums(info, all_of([one, one_recv]), all_of([two, two_recv]))
    small_r, one = lax.optimization_barrier((small_r, one))
    one = gather_quarters(swap_far(info, one))
    two = gather_quarters(swap_far(info, two))
    small_g = small_g + small_r
    for mask in masks_of(lax.axis_size("rep"))[2:]:
        small_g = small_g + swap(small_g, "rep", mask)
    conv_g = lax.dynamic_slice_in_dim(small_g[: taps + 1], me * chans, chans, 1)
    per = heads // n
    head_g = lax.dynamic_slice_in_dim(small_g[:3], n * chans + me * per, per, 1)
    sub = inner // n // r
    out_quarter = sub * (width // LANES) // 4
    gate_quarter = inner // LANES // 4
    one_cols, two_cols = gx_one.shape[1], gx_two.shape[1] + gbcdt.shape[1]
    gw_out, gain_sums = call_assemble(info, [wide], ((0, out_quarter, 0, sub),), w_out, False)
    gw_in, pre_sums = call_assemble(
        info, [wide, one, two],
        ((0, gate_quarter, out_quarter, 1), (inner, one_cols // LANES // 4, 0, 1),
         (inner + one_cols, two_cols // LANES // 4, 0, 1)), weights_t, True)
    grad_pre = pre_sums[0] / pre_gain.astype(F32)
    grad_gain = gain_sums[:, 0] / norm_gain.astype(F32)
    return (res.reshape(inputs.shape), grad_in.reshape(inputs.shape), grad_pre, gw_in.T, conv_g[:taps], conv_g[taps],
            head_g[0], head_g[1], head_g[2], grad_gain, gw_out)


def solution(mesh):
    data = P(None, ("rep", "fsdp"), None, None)
    vec = P("fsdp")
    in_specs = (data, data, P(None, ("rep", "fsdp")), vec, P("fsdp", None), P(None, "fsdp"), vec, vec, vec, vec, vec,
                P("fsdp", None))
    out_specs = (data, data, vec, P("fsdp", None), P(None, "fsdp"), vec, vec, vec, vec, vec, P("fsdp", None))

    return jax.shard_map(on_device, mesh=mesh, in_specs=in_specs, out_specs=out_specs, check_vma=False)
```
